32 devices in a mesh: src: 2 (over core), brick: 16 (over z, y, x).
Axes of the slice: x: 2, y: 2, z: 4, core: 2. Of those that a mesh axis runs over, the one named last changes fastest.
Arguments:
- slowness: float32 [64, 64, 128], P('brick'), may hold values from 0.5 to 2
- source_x: int32 [4], P('src'), may hold values from 0 to 63
- source_y: int32 [4], P('src'), may hold values from 0 to 63
- source_z: int32 [4], P('src'), may hold values from 0 to 127
- station_x: int32 [2048], replicated, may hold values from 0 to 63
- station_y: int32 [2048], replicated, may hold values from 0 to 63
- station_z: int32 [2048], replicated, may hold values from 0 to 127
- observed: float32 [4, 2048], P('src'), may hold values from 0 to 4
Outputs:
- kernel: float32 [64, 64, 128], P('brick', 'src')
- arrivals: float32 [4, 2048], P('src', 'brick')
The draws below stay inside these ranges and needn't reach their ends.
All inputs are finite; a program needn't handle non-finite values.
Results may differ from the reference program's by a relative error of at most 0.0003.
Values sent between devices are 32-bit elements; how exact they have to be, the bound alone decides.
A program may use at most 128 MiB of HBM per device.

```python
import math
import jax
import jax.numpy as jnp
from jax import lax

NY = 64
NZ = 128
REC = 2048
ITERS = 16
NX = 64
SOURCES = 4


def touch_ends(values, key, low, high):
    extent = values.shape
    spot = [jax.random.randint(jax.random.fold_in(key, axis), (), 0, extent[axis]) for axis in range(len(extent))]
    values = values.at[tuple(spot)].set(low)
    longest = extent.index(max(extent))
    spot[longest] = (spot[longest] + 1) % extent[longest]
    return values.at[tuple(spot)].set(high)


def steps_of(key, extent, shards, low, largest):
    def one(position, parts):
        draws = jax.random.uniform(jax.random.fold_in(jax.random.fold_in(key, 6), position), (parts,), jnp.float32, low / len(shards), largest / len(shards))
        return jnp.repeat(jnp.exp(draws), extent[position] // parts).reshape((-1,) + (1,) * (len(extent) - position - 1))

    loudness = one(*shards[0])
    for cut in shards[1:]:
        loudness = loudness * one(*cut)
    return loudness


def setup_inputs(seed: int = 0) -> dict:
    key_list = jax.random.split(jax.random.key(seed), 9)
    return {
        "slowness": jnp.clip(jnp.exp(math.log(2.0) - 1.3862944 * jax.random.uniform(key_list[0], (NX, NY, NZ), jnp.float32) ** steps_of(key_list[0], (NX, NY, NZ), ((0, 16),), -0.2, 0.2)), 0.5, 2.0),
        "source_x": touch_ends(jax.random.randint(key_list[1], (SOURCES,), 0, NX), jax.random.fold_in(key_list[1], 1), 0, NX - 1).astype(jnp.int32),
        "source_y": touch_ends(jax.random.randint(key_list[2], (SOURCES,), 0, NY), jax.random.fold_in(key_list[2], 1), 0, NY - 1).astype(jnp.int32),
        "source_z": touch_ends(jax.random.randint(key_list[3], (SOURCES,), 0, NZ), jax.random.fold_in(key_list[3], 1), 0, NZ - 1).astype(jnp.int32),
        "station_x": touch_ends(jax.random.randint(key_list[4], (REC,), 0, NX), jax.random.fold_in(key_list[4], 1), 0, NX - 1).astype(jnp.int32),
        "station_y": touch_ends(jax.random.randint(key_list[5], (REC,), 0, NY), jax.random.fold_in(key_list[5], 1), 0, NY - 1).astype(jnp.int32),
        "station_z": touch_ends(jax.random.randint(key_list[6], (REC,), 0, NZ), jax.random.fold_in(key_list[6], 1), 0, NZ - 1).astype(jnp.int32),
        "observed": jnp.clip(4.0 * jax.random.uniform(key_list[7], (SOURCES, REC), jnp.float32) ** steps_of(key_list[7], (SOURCES, REC), ((0, 2),), -0.2, 0.2), 0.0, 4.0),
    }


spacing = 0.015625
big_value = 1000000.0
start_slowness = 2.0

def neighbours(padded):
    return [padded[2:, 1:-1, 1:-1], padded[:-2, 1:-1, 1:-1], padded[1:-1, 2:, 1:-1], padded[1:-1, :-2, 1:-1], padded[1:-1, 1:-1, 2:], padded[1:-1, 1:-1, :-2]]

def reference(slowness, source_x, source_y, source_z, station_x, station_y, station_z, observed):
    slow_pad = jnp.pad(slowness, 1, constant_values=1.0)
    costs = [spacing * 0.5 * (slowness + other) for other in neighbours(slow_pad)]
    grid_x = jnp.arange(NX, dtype=jnp.float32)[:, None, None]
    grid_y = jnp.arange(NY, dtype=jnp.float32)[None, :, None]
    grid_z = jnp.arange(NZ, dtype=jnp.float32)[None, None, :]
    flat = ((station_x * NY + station_y) * NZ + station_z).astype(jnp.int32)

    def forward_sweep(step, times):
        padded = jnp.pad(times, 1, constant_values=big_value)
        fresh = times
        for cost, other in zip(costs, neighbours(padded)):
            fresh = jnp.minimum(fresh, other + cost)
        return fresh

    def one_source(total, inputs):
        sx, sy, sz, seen = inputs
        dist = (grid_x - sx.astype(jnp.float32)) ** 2 + (grid_y - sy.astype(jnp.float32)) ** 2 + (grid_z - sz.astype(jnp.float32)) ** 2
        times = start_slowness * spacing * jnp.sqrt(dist)
        times = lax.fori_loop(0, ITERS, forward_sweep, times)
        arrive = times.reshape(-1)[flat]
        source = jnp.zeros((NX * NY * NZ,), jnp.float32).at[flat].add(arrive - seen).reshape(NX, NY, NZ)
        low_pad = jnp.pad(times, 1, constant_values=-big_value)
        weights = [jnp.maximum(other - times, 0.0) / spacing for other in neighbours(low_pad)]
        denom = 1.0 + weights[0] + weights[1] + weights[2] + weights[3] + weights[4] + weights[5]

        def adjoint_sweep(step, field):
            padded = jnp.pad(field, 1)
            acc = source
            for weight, other in zip(weights, neighbours(padded)):
                acc = acc + weight * other
            return acc / denom
        field = lax.fori_loop(0, ITERS, adjoint_sweep, jnp.zeros((NX, NY, NZ), jnp.float32))
        return (total + field, arrive)
    summed, arrivals = lax.scan(one_source, jnp.zeros((NX, NY, NZ), jnp.float32), (source_x, source_y, source_z, observed))
    return (slowness * summed, arrivals)
```

```python
import functools

import jax
import jax.numpy as jnp
from jax import lax
from jax.experimental import pallas as pl
from jax.experimental.pallas import tpu as pltpu
from jax.sharding import PartitionSpec as P

ITERS = 16

spacing = 0.015625
big_value = 1000000.0
start_slowness = 2.0
half_step = 0.5 * spacing
LOW = 4
GATHER_VMEM = 24 << 20
SOLVE_VMEM = 44 << 20
FINISH_VMEM = 8 << 20
TALLY = 512

VMEM = pl.BlockSpec(memory_space=pltpu.VMEM)
SMEM = pl.BlockSpec(memory_space=pltpu.SMEM)
HBM = pl.BlockSpec(memory_space=pltpu.HBM)
MESH = pl.DeviceIdType.MESH


def remote(src, dst, send_sem, recv_sem, core, brick):
    return pltpu.make_async_remote_copy(
        src_ref=src,
        dst_ref=dst,
        send_sem=send_sem,
        recv_sem=recv_sem,
        device_id={"src": core, "brick": brick},
        device_id_type=MESH,
    )


def gather_kernel(
    bricks,
    slow_ref,
    sx_ref,
    sy_ref,
    sz_ref,
    stx_ref,
    sty_ref,
    stz_ref,
    obs_ref,
    full_ref,
    tally_ref,
    code_ref,
    spot_ref,
    table,
    line_sem,
    send_sem,
    recv_sem,
    twin_sem,
    own_sem,
    stx_buf,
    sty_buf,
    stz_buf,
    seen_buf,
    sx_buf,
    sy_buf,
    sz_buf,
    in_sem,
    word_send,
    word_recv,
):
    depth = slow_ref.shape[0]
    half = depth // 2
    lines = bricks // LOW
    me = lax.axis_index("brick")
    core = lax.axis_index("src")
    h = lax.rem(core, 2)
    twin = core + 1 - 2 * h
    line = me // LOW
    place = lax.rem(me, LOW)
    bit_x = lax.rem(me, 2)
    bit_y = lax.rem(me // 2, 2)
    flip_x = 1 - 2 * bit_x
    flip_y = 2 - 4 * bit_y
    first = me + flip_x * (1 - h) + flip_y * h
    second = me + flip_y * (1 - h) + flip_x * h
    corner = me + flip_x + flip_y
    owner = place // 2 == h
    local = lax.rem(place, 2)

    barrier = pltpu.get_barrier_semaphore()

    def greet(c, b):
        pl.semaphore_signal(barrier, inc=1, device_id={"src": c, "brick": b}, device_id_type=MESH)

    greet(twin, me)
    greet(core, first)
    greet(core, second)
    for k in range(1, lines):
        pl.when(line >= k)(lambda k=k: greet(core, me - LOW * k))
        pl.when(line + k < lines)(lambda k=k: greet(core, me + LOW * k))

    stations = [
        pltpu.make_async_copy(src, dst, in_sem.at[k])
        for k, (src, dst) in enumerate(((stx_ref, stx_buf), (sty_ref, sty_buf), (stz_ref, stz_buf)))
    ]
    spots = [
        pltpu.make_async_copy(src, dst, in_sem.at[3 + k])
        for k, (src, dst) in enumerate(((sx_ref, sx_buf), (sy_ref, sy_buf), (sz_ref, sz_buf)))
    ]
    seen_copy = pltpu.make_async_copy(obs_ref, seen_buf, in_sem.at[6])
    for load in stations:
        load.start()

    @pl.when(owner)
    def _():
        for load in spots:
            load.start()
        seen_copy.start()

    def piece(q, part):
        return full_ref.at[pl.ds(q * depth + part * half, half)]

    def copy(kind, q, brick, own=False):
        src = slow_ref.at[pl.ds(h * half, half)] if own else piece(q, h)
        return remote(src, piece(q, h), send_sem.at[kind, q], recv_sem.at[q], core, brick)

    def twin_copy(q):
        return remote(piece(q, h), piece(q, h), send_sem.at[2, q], twin_sem.at[q], twin, me)

    def along(k, up):
        dst = piece(me, h)
        src = slow_ref.at[pl.ds(h * half, half)]
        brick = me + LOW * k if up else me - LOW * k
        return remote(src, dst, line_sem.at[int(up), k], recv_sem.at[me], core, brick)

    def own_line(k, wait):
        def go(up):
            c = along(k, up)
            c.wait_send() if wait else c.start()

        pl.when(line >= k)(lambda: go(False))
        pl.when(line + k < lines)(lambda: go(True))

    def sends(q, own, wait):
        for kind, brick in ((0, first), (1, second)):
            c = copy(kind, q, brick, own)
            c.wait_send() if wait else c.start()

    own_copy = pltpu.make_async_copy(slow_ref, full_ref.at[pl.ds(me * depth, depth)], own_sem)
    seen_send = remote(obs_ref, seen_buf, word_send.at[0], word_recv.at[0], twin, me)
    spot_send = remote(spot_ref, spot_ref, word_send.at[1], word_recv.at[1], twin, me)

    pl.semaphore_wait(barrier, lines + 2)
    pl.when(owner)(seen_send.start)
    for k in range(1, lines):
        own_line(k, False)
        if k == 1:
            sends(me, True, False)
    own_copy.start()

    def arrived(q):
        remote(piece(q, h), piece(q, h), send_sem.at[0, q], recv_sem.at[q], core, first).wait_recv()

    def on_line(base, i, act):
        pl.when((i < lines) & (line >= i))(lambda: act(base - LOW * i, -1))
        pl.when((i < lines) & (line + i < lines))(lambda: act(base + LOW * i, 1))

    def both(base, i, act):
        pl.when(i == 0)(lambda: act(base, 0))
        pl.when(i > 0)(lambda: on_line(base, i, act))

    def from_line(wait):
        def act(q, side):
            if not wait:
                arrived(q)
            sends(q, False, wait)
            c = twin_copy(q)
            c.wait_send() if wait else c.start()

        return act

    def from_first(wait):
        def act(q, side):
            if not wait:
                arrived(q)
            c = copy(1, q, second)
            c.wait_send() if wait else c.start()
            c = twin_copy(q)
            c.wait_send() if wait else c.start()

        return act

    def from_second(wait):
        def act(q, side):
            if not wait:
                arrived(q)
            c = twin_copy(q)
            c.wait_send() if wait else c.start()

        return act

    def turn(i, wait):
        on_line(me, i, from_line(wait))
        both(first, i - 1, from_first(wait))
        both(second, i - 1, from_second(wait))
        pl.when(i >= 2)(lambda: both(corner, i - 2, from_second(wait)))

    @pl.when(owner)
    def _():
        for load in spots:
            load.wait()
        sub = lax.broadcasted_iota(jnp.int32, spot_ref.shape, 0)
        spot_ref[...] = jnp.where(
            sub == 0, sx_buf[local], jnp.where(sub == 1, sy_buf[local], sz_buf[local])
        )

    for load in stations:
        load.wait()
    grid_x, cells_y, cells_z = full_ref.shape
    rows = cells_y // 8
    shift = rows.bit_length() - 1
    ring = grid_x // 2
    centre = line * (LOW * depth) + LOW * depth // 2
    sty = sty_buf[...]
    stz = stz_buf[...]
    stx = stx_buf[...]
    away = stx - centre
    away = jnp.where(away < 0, away + grid_x, away)
    upper = away < ring
    step_x = jnp.where(upper, away, grid_x - 1 - away)
    row = (step_x * rows + (sty & (rows - 1))) * 8 + (sty >> shift)
    column = jnp.where(upper, cells_z // 2, 0) + (stz >> 1)
    column = jnp.where(((stx + sty + stz) & 1) == h, column, -1)
    code_ref[0] = row
    code_ref[1] = column
    rec = row.shape[1]
    hit = lax.broadcasted_iota(jnp.int32, (cells_z, rec), 0) == column

    pl.when(owner)(seen_copy.wait)
    pl.when(owner)(spot_send.start)
    pl.when(jnp.logical_not(owner))(seen_send.wait_recv)
    seen = seen_buf[pl.ds(local, 1), :] * (1.0 / spacing)
    hi = seen.astype(jnp.bfloat16).astype(jnp.float32)
    rest = seen - hi
    mid = rest.astype(jnp.bfloat16).astype(jnp.float32)
    lo = rest - mid
    for part, value in enumerate((jnp.ones_like(seen), hi, mid, lo)):
        table[pl.ds(part * cells_z, cells_z), :] = jnp.where(hit, value, 0.0).astype(jnp.bfloat16)

    tiles = TALLY // 8
    blocks = tally_ref.shape[1] // tiles

    def tally(step):
        rows_of = lax.broadcasted_iota(jnp.int32, (TALLY, rec), 0) + step * TALLY
        pick = jnp.where(rows_of == row, 1.0, 0.0).astype(jnp.bfloat16)
        got = lax.dot_general(
            pick, table[...], (((1,), (1,)), ((), ())), preferred_element_type=jnp.float32
        )
        spot = pl.ds(step * tiles, tiles)
        tally_ref[0, spot] = got[:, :cells_z].reshape(tiles, 8, cells_z)
        total = got[:, cells_z : 2 * cells_z] + (
            got[:, 2 * cells_z : 3 * cells_z] + got[:, 3 * cells_z :]
        )
        tally_ref[1, spot] = total.reshape(tiles, 8, cells_z)

    rounds = lines + 1
    tally_send = remote(
        tally_ref.at[pl.ds(0, 2)], tally_ref.at[pl.ds(2, 2)], word_send.at[2], word_recv.at[2], twin, me
    )

    @pl.loop(0, max(rounds, blocks + 1))
    def _(step):
        pl.when(step < blocks)(lambda: tally(step))
        pl.when(step < rounds)(lambda: turn(step + 1, False))
        pl.when(step == blocks)(tally_send.start)

    own_copy.wait()
    sends(me, True, True)
    for k in range(1, lines):
        own_line(k, True)

    @pl.loop(1, lines + 2)
    def _(i):
        turn(i, True)

    @pl.loop(0, bricks)
    def _(q):
        @pl.when(q != me)
        def _():
            remote(piece(q, 1 - h), piece(q, 1 - h), send_sem.at[2, q], twin_sem.at[q], twin, me).wait_recv()

    tally_send.wait()

    @pl.when(owner)
    def _():
        seen_send.wait_send()
        spot_send.wait_send()

    pl.when(jnp.logical_not(owner))(spot_send.wait_recv)


def solve_kernel(
    depth,
    cores,
    code_ref,
    spot_ref,
    full_ref,
    tally_ref,
    slots_ref,
    got_ref,
    chain,
    other,
    chain_cost,
    other_cost,
    twin_time,
    chain_weight,
    other_weight,
    chain_supply,
    other_supply,
    chain_field,
    other_field,
    packed,
    picked,
    part,
    code,
    code_sem,
    time_send,
    time_recv,
    send_sem,
    recv_sem,
    part_send,
    part_recv,
    self_sem,
):
    grid_x, cells_y, cells_z = full_ref.shape
    rows = cells_y // 8
    ring = grid_x // 2
    block = LOW * depth
    half = block // 2
    span = half + ITERS
    brick = lax.axis_index("brick")
    core = lax.axis_index("src")
    h = lax.rem(core, 2)
    twin = core + 1 - 2 * h
    group = brick // LOW
    place = lax.rem(brick, LOW)
    base = group * LOW
    peers = LOW * cores
    mine = core * LOW + place
    centre = group * block + half
    half_z = cells_z // 2

    barrier = pltpu.get_barrier_semaphore()

    def peer(k):
        t = lax.rem(mine + k, peers)
        return t // LOW, base + lax.rem(t, LOW), lax.rem(t, LOW)

    for k in range(1, peers):
        c, b, _ = peer(k)
        pl.semaphore_signal(barrier, inc=1, device_id={"src": c, "brick": b}, device_id_type=MESH)

    share = got_ref.shape[-1]
    quarter = picked.shape[0]
    load_code = pltpu.make_async_copy(code_ref.at[0], code, code_sem)
    load_code.start()

    lane = lax.broadcasted_iota(jnp.int32, (8, cells_z), 1)
    sub = lax.broadcasted_iota(jnp.int32, (8, cells_z), 0)
    sub_first = sub == 0
    sub_last = sub == 7
    upper = lane >= half_z
    inner = jnp.where(upper, lane - half_z, lane)
    parity = [lax.rem(q + h, 2) for q in range(2)]
    cell_z = [inner * 2 + jnp.where(upper, 1 - p, p) for p in parity]
    from_low = [(lane & 1) == p for p in parity]
    slide = [inner + jnp.where(upper, 1, -1) * (1 - 2 * p) for p in parity]
    edge_z = [(s < 0) | (s >= half_z) for s in slide]
    far = [jnp.where(upper, half_z, 0) + jnp.clip(s, 0, half_z - 1) for s in slide]

    def slot(i, v):
        return (i + 1) * rows + v

    sx = spot_ref[0:1, :]
    sy = spot_ref[1:2, :]
    sz = spot_ref[2:3, :]
    unit = (start_slowness * spacing) ** 2
    flat = []
    for q in range(2):
        dz = (cell_z[q] - sz).astype(jnp.float32)
        dz = dz * dz
        for v in range(rows):
            dy = (sub * rows + v - sy).astype(jnp.float32)
            flat.append((dy * dy + dz) * unit)

    @pl.loop(0, ring // 2)
    def _(pair):
        for j in range(2):
            i = pair * 2 + j
            x_low = centre - 1 - i
            x_low = jnp.where(x_low < 0, x_low + grid_x, x_low)
            x_high = centre + i
            x_high = jnp.where(x_high >= grid_x, x_high - grid_x, x_high)
            dx = (jnp.where(upper, x_high, x_low) - sx).astype(jnp.float32)
            dx = dx * dx * unit
            for v in range(rows):
                q = (j + 1 + v) % 2
                low = full_ref[x_low, pl.ds(v, 8, stride=rows), :]
                high = full_ref[x_high, pl.ds(v, 8, stride=rows), :]
                for field, cost, k, natural in (
                    (chain, chain_cost, q, jnp.where(from_low[q], low, high)),
                    (other, other_cost, 1 - q, jnp.where(from_low[q], high, low)),
                ):
                    slow = jnp.take_along_axis(natural, cell_z[k], axis=1)
                    square = dx + flat[k * rows + v]
                    start = square * lax.rsqrt(jnp.maximum(square, unit * 0.5))
                    cost[i * rows + v] = (2.0 * half_step) * slow
                    field[slot(i, v)] = start + half_step * slow

    cuts = {
        b: jnp.where(upper, grid_x - centre, centre) == b for b in range(half, ring, half) if (b // half) % 2
    }

    def swing(one):
        return pltpu.roll(one, half_z, 1)

    def y_up(cur, v):
        return cur[v + 1] if v + 1 < rows else pltpu.roll(cur[0], 7, 0)

    def y_down(cur, v):
        return cur[v - 1] if v else pltpu.roll(cur[rows - 1], 1, 0)

    def sweep(dst, cost, src, turned):
        for i in range(ring):
            cur = [src[slot(i, v)] for v in range(rows)]
            for v in range(rows):
                q = (i + 1 + v) % 2
                before = src[slot(i - 1, v)] if i else swing(cur[v])
                after = src[slot(i + 1, v)] if i + 1 < ring else swing(cur[v])
                if i in cuts:
                    before = jnp.where(cuts[i], big_value, before)
                if i + 1 in cuts:
                    after = jnp.where(cuts[i + 1], big_value, after)
                up = y_up(cur, v)
                down = y_down(cur, v)
                if v + 1 == rows:
                    up = jnp.where(sub_last, big_value, up)
                if v == 0:
                    down = jnp.where(sub_first, big_value, down)
                across = jnp.take_along_axis(cur[v], far[q ^ turned], axis=1)
                low = jnp.minimum(
                    jnp.minimum(jnp.minimum(before, after), jnp.minimum(up, down)),
                    jnp.minimum(cur[v], across),
                )
                dst[slot(i, v)] = jnp.minimum(dst[slot(i, v)], low + cost[i * rows + v])

    assert ITERS % 2 == 0

    @pl.loop(0, ITERS // 2)
    def _(_step):
        sweep(other, other_cost, chain, 1)
        sweep(chain, chain_cost, other, 0)

    @pl.loop(0, ring)
    def _(i):
        for v in range(rows):
            chain[slot(i, v)] = (chain[slot(i, v)] - 0.5 * chain_cost[i * rows + v]) * (1.0 / spacing)

    for v in range(rows):
        chain[slot(-1, v)] = swing(chain[slot(0, v)])

    pl.semaphore_wait(barrier, peers - 1)
    reach = span + 2
    time_copy = remote(
        chain.at[pl.ds(0, reach * rows)], twin_time, time_send, time_recv, twin, brick
    )
    time_copy.start()

    load_code.wait()
    unroll = 16

    @pl.loop(0, quarter // unroll)
    def _(n):
        for j in range(unroll):
            r = n * unroll + j
            at = code[0, group * quarter + r]
            picked[pl.ds(r, 1), :] = chain[(at >> 3) + rows, pl.ds(at & 7, 1), :]

    column = code_ref[1, :, pl.ds(pl.multiple_of(group * quarter, 128), quarter)]
    turned = jnp.transpose(picked[...])
    here = lax.broadcasted_iota(jnp.int32, turned.shape, 0) == column
    arrived = jnp.sum(jnp.where(here, turned, 0.0), axis=0, keepdims=True) * spacing
    for k in range(LOW):
        part[k] = arrived[:, k * share : (k + 1) * share]

    for v in range(rows):
        chain_field[slot(span - 2, v)] = jnp.zeros((8, cells_z), jnp.float32)
        chain_field[slot(span - 1, v)] = jnp.zeros((8, cells_z), jnp.float32)
        chain_field[slot(span, v)] = jnp.zeros((8, cells_z), jnp.float32)
        other_field[slot(span, v)] = jnp.zeros((8, cells_z), jnp.float32)

    time_copy.wait_recv()
    bound = jnp.where(upper, grid_x - centre, centre)

    def weigh(at, i, own, theirs, weight, supply, field, tally, turned):
        cur = [theirs[slot(at, v)] for v in range(rows)]
        cut_before = bound == at
        cut_after = bound == at + 1
        for v in range(rows):
            q = (i + 1 + v) % 2
            one = own[slot(at, v)]

            def gain(value):
                return jnp.maximum(value - one, 0.0)

            before = gain(theirs[slot(at - 1, v)])
            after = gain(theirs[slot(at + 1, v)])
            if i % half == 0:
                before = jnp.where(cut_before, 0.0, before)
            if (i + 1) % half == 0:
                after = jnp.where(cut_after, 0.0, after)
            up = gain(y_up(cur, v))
            down = gain(y_down(cur, v))
            if v + 1 == rows:
                up = jnp.where(sub_last, 0.0, up)
            if v == 0:
                down = jnp.where(sub_first, 0.0, down)
            k = q ^ turned
            across = jnp.where(edge_z[k], 0.0, gain(jnp.take_along_axis(cur[v], far[k], axis=1)))
            parts = (before, after, down, up, gain(cur[v]), across)
            total = ((parts[0] + parts[1]) + (parts[2] + parts[3])) + (parts[4] + parts[5])
            inverse = 1.0 / (1.0 + total)
            spot = at * rows + v
            for n, gained in enumerate(parts):
                weight[n, spot] = gained * inverse
            value = (tally_ref[tally, spot] * one - tally_ref[tally + 1, spot]) * inverse
            supply[spot] = value
            if turned:
                field[slot(at, v)] = value

    @pl.loop(0, span // half)
    def _(chunk):
        for i in range(half):
            at = chunk * half + i
            weigh(at, i, twin_time, chain, other_weight, other_supply, other_field, 2, 1)
            weigh(at, i, chain, twin_time, chain_weight, chain_supply, chain_field, 0, 0)

    for v in range(rows):
        other_field[slot(-1, v)] = swing(other_field[slot(0, v)])

    def backward(count, dst, weight, supply, src, turned):
        for i in range(count):
            cur = [src[slot(i, v)] for v in range(rows)]
            for v in range(rows):
                q = (i + 1 + v) % 2
                spot = i * rows + v
                before = src[slot(i - 1, v)] if i else swing(cur[v])
                acc = supply[spot] + weight[0, spot] * before
                acc = acc + weight[1, spot] * src[slot(i + 1, v)]
                side = weight[2, spot] * y_down(cur, v) + weight[3, spot] * y_up(cur, v)
                across = jnp.take_along_axis(cur[v], far[q ^ turned], axis=1)
                acc = (acc + side) + (weight[4, spot] * cur[v] + weight[5, spot] * across)
                dst[slot(i, v)] = acc

    def rounds(first, times):
        count = half + ITERS - first

        @pl.loop(0, times)
        def _(_step):
            backward(count, chain_field, chain_weight, chain_supply, other_field, 0)
            backward(count - 1, other_field, other_weight, other_supply, chain_field, 1)

    rounds(2, 3)
    rounds(8, 2)
    rounds(12, 2)
    backward(half, chain_field, chain_weight, chain_supply, other_field, 0)

    for k in range(LOW):
        for t in range(0, depth, 2):
            low_side = k < LOW // 2
            near, next_to = (
                (half - 1 - (k * depth + t + n)) if low_side else (k * depth + t + n - half) for n in range(2)
            )
            for v in range(rows):
                a = chain_field[slot(near, v)]
                b = chain_field[slot(next_to, v)]
                both = jnp.where(upper, swing(b), a) if low_side else jnp.where(upper, b, swing(a))
                packed[k, t // 2, pl.ds(v, 8, stride=rows), :] = both

    keep = slots_ref.shape[2]

    def ship(k):
        c, b, p = peer(k)
        return remote(
            packed.at[p, :, pl.ds(c * keep, keep)], slots_ref.at[mine], send_sem.at[k], recv_sem.at[mine], c, b
        )

    for k in range(1, peers):
        ship(k).start()
    stay = pltpu.make_async_copy(
        packed.at[place, :, pl.ds(core * keep, keep)], slots_ref.at[mine], self_sem
    )
    stay.start()

    target = core - h + place // 2
    local = lax.rem(place, 2)

    def word(k):
        return remote(
            part.at[k], got_ref.at[local, h], part_send.at[k], part_recv.at[local, h], target, base + k
        )

    def home(k):
        return (target == core) & (place == k)

    for k in range(LOW):
        pl.when(jnp.logical_not(home(k)))(word(k).start)

        @pl.when(home(k))
        def _():
            got_ref[local, h] = part[k]

    def word_in(n, side):
        return remote(
            part.at[0], got_ref.at[n, side], part_send.at[0], part_recv.at[n, side], core, brick
        )

    for n in range(2):
        for side in range(2):
            from_me = (place == 2 * h + n) & (h == side)
            pl.when(jnp.logical_not(from_me))(word_in(n, side).wait_recv)
    for k in range(1, peers):
        m = lax.rem(mine + k, peers)
        remote(
            packed.at[0, :, pl.ds(0, keep)], slots_ref.at[m], send_sem.at[k], recv_sem.at[m], core, brick
        ).wait_recv()
    for k in range(1, peers):
        ship(k).wait_send()
    for k in range(LOW):
        pl.when(jnp.logical_not(home(k)))(word(k).wait_send)
    stay.wait()
    time_copy.wait_send()


def finish_kernel(cores, slots_ref, got_ref, full_ref, out_ref, arr_ref):
    depth, keep, cells_z = out_ref.shape
    half_z = cells_z // 2
    first = lax.axis_index("brick") * depth
    row = pl.multiple_of(lax.axis_index("src") * keep, 8)
    lane = lax.broadcasted_iota(jnp.int32, (8, cells_z), 1)
    sub = lax.broadcasted_iota(jnp.int32, (8, cells_z), 0)
    upper = lane >= half_z
    plain = ((sub + jnp.where(upper, 1, 0)) & 1) == 0
    join = (lane & 1) * half_z + (lane >> 1)
    for t in range(depth // 2):
        for y in range(0, keep, 8):
            sums = []
            for colour in range(2):
                total = None
                for c in range(colour, cores, 2):
                    for k in range(LOW):
                        one = slots_ref[c * LOW + k, t, pl.ds(y, 8), :]
                        total = one if total is None else total + one
                sums.append(total)
            even = jnp.where(plain, sums[0], sums[1])
            odd = jnp.where(plain, sums[1], sums[0])
            moved = pltpu.roll(jnp.where(upper, even, odd), half_z, 1)
            for n, packed in enumerate((jnp.where(upper, moved, even), jnp.where(upper, odd, moved))):
                value = jnp.take_along_axis(packed, join, axis=1)
                slow = full_ref[first + 2 * t + n, pl.ds(row + y, 8), :]
                out_ref[2 * t + n, pl.ds(y, 8), :] = (slow * spacing) * value
    for n in range(2):
        arr_ref[pl.ds(n, 1), :] = got_ref[n, 0] + got_ref[n, 1]


def per_device(slowness, source_x, source_y, source_z, station_x, station_y, station_z, observed):
    bricks = lax.axis_size("brick")
    cores = lax.axis_size("src")
    depth, cells_y, cells_z = slowness.shape
    grid_x = depth * bricks
    rec = station_x.shape[0]
    rows = cells_y // 8
    ring = grid_x // 2
    half = LOW * depth // 2
    span = half + ITERS
    assert source_x.shape[0] == 2 and bricks % LOW == 0 and cores % 2 == 0
    assert half % 2 == 0 and span % half == 0 and span + 1 <= ring and (span * rows * 8) % TALLY == 0
    f32 = jnp.float32
    i32 = jnp.int32

    full, tally, code, spot = pl.pallas_call(
        functools.partial(gather_kernel, bricks),
        name="gather",
        out_shape=(
            jax.ShapeDtypeStruct((grid_x, cells_y, cells_z), f32),
            jax.ShapeDtypeStruct((4, span * rows, 8, cells_z), f32),
            jax.ShapeDtypeStruct((2, 1, rec), i32),
            jax.ShapeDtypeStruct((8, cells_z), i32),
        ),
        in_specs=[HBM] * 8,
        out_specs=(VMEM, VMEM, VMEM, VMEM),
        scratch_shapes=[
            pltpu.VMEM((4 * cells_z, rec), jnp.bfloat16),
            pltpu.SemaphoreType.DMA((2, bricks // LOW)),
            pltpu.SemaphoreType.DMA((3, bricks)),
            pltpu.SemaphoreType.DMA((bricks,)),
            pltpu.SemaphoreType.DMA((bricks,)),
            pltpu.SemaphoreType.DMA,
            pltpu.VMEM((1, rec), i32),
            pltpu.VMEM((1, rec), i32),
            pltpu.VMEM((1, rec), i32),
            pltpu.VMEM(observed.shape, f32),
            pltpu.SMEM((2,), i32),
            pltpu.SMEM((2,), i32),
            pltpu.SMEM((2,), i32),
            pltpu.SemaphoreType.DMA((7,)),
            pltpu.SemaphoreType.DMA((3,)),
            pltpu.SemaphoreType.DMA((3,)),
        ],
        compiler_params=pltpu.CompilerParams(
            collective_id=0, has_side_effects=True, vmem_limit_bytes=GATHER_VMEM
        ),
    )(
        slowness,
        source_x,
        source_y,
        source_z,
        station_x[None],
        station_y[None],
        station_z[None],
        observed,
    )

    share = rec // bricks
    quarter = share * LOW
    keep = cells_y // cores
    layer = (rows, 8, cells_z)
    ring_shape = ((ring + 2) * rows, 8, cells_z)
    slots, got = pl.pallas_call(
        functools.partial(solve_kernel, depth, cores),
        name="solve",
        out_shape=(
            jax.ShapeDtypeStruct((LOW * cores, depth // 2, keep, cells_z), f32),
            jax.ShapeDtypeStruct((2, 2, 1, share), f32),
        ),
        in_specs=[VMEM] * 4,
        out_specs=(VMEM, VMEM),
        scratch_shapes=[
            pltpu.VMEM(ring_shape, f32),
            pltpu.VMEM(ring_shape, f32),
            pltpu.VMEM((ring * rows, 8, cells_z), f32),
            pltpu.VMEM((ring * rows, 8, cells_z), f32),
            pltpu.VMEM(((span + 2) * rows, 8, cells_z), f32),
            pltpu.VMEM((6, span * rows, 8, cells_z), f32),
            pltpu.VMEM((6, span * rows, 8, cells_z), f32),
            pltpu.VMEM((span * rows, 8, cells_z), f32),
            pltpu.VMEM((span * rows, 8, cells_z), f32),
            pltpu.VMEM(((span + 2) * rows, 8, cells_z), f32),
            pltpu.VMEM(((span + 2) * rows, 8, cells_z), f32),
            pltpu.VMEM((LOW, depth // 2, cells_y, cells_z), f32),
            pltpu.VMEM((quarter, cells_z), f32),
            pltpu.VMEM((LOW, 1, share), f32),
            pltpu.SMEM((1, rec), i32),
            pltpu.SemaphoreType.DMA,
            pltpu.SemaphoreType.DMA,
            pltpu.SemaphoreType.DMA,
            pltpu.SemaphoreType.DMA((LOW * cores,)),
            pltpu.SemaphoreType.DMA((LOW * cores,)),
            pltpu.SemaphoreType.DMA((LOW,)),
            pltpu.SemaphoreType.DMA((2, 2)),
            pltpu.SemaphoreType.DMA,
        ],
        compiler_params=pltpu.CompilerParams(
            collective_id=1, has_side_effects=True, vmem_limit_bytes=SOLVE_VMEM
        ),
    )(code, spot, full, tally)

    return tuple(
        pl.pallas_call(
            functools.partial(finish_kernel, cores),
            name="finish",
            out_shape=(
                jax.ShapeDtypeStruct((depth, keep, cells_z), f32),
                jax.ShapeDtypeStruct((2, share), f32),
            ),
            in_specs=[VMEM] * 3,
            compiler_params=pltpu.CompilerParams(vmem_limit_bytes=FINISH_VMEM),
        )(slots, got, full)
    )


def solution(mesh):
    in_specs = (P("brick", None, None), P("src"), P("src"), P("src"), P(), P(), P(), P("src", None))
    out_specs = (P("brick", "src", None), P("src", "brick"))
    return jax.shard_map(
        per_device, mesh=mesh, in_specs=in_specs, out_specs=out_specs, check_vma=False
    )
```

```python
import functools

import jax
import jax.numpy as jnp
from jax import lax
from jax.experimental import pallas as pl
from jax.experimental.pallas import tpu as pltpu
from jax.sharding import PartitionSpec as P

ITERS = 16

spacing = 0.015625
big_value = 1000000.0
start_slowness = 2.0
half_step = 0.5 * spacing
LOW = 4
GATHER_VMEM = 24 << 20
SOLVE_VMEM = 44 << 20
FINISH_VMEM = 8 << 20
TALLY = 512

VMEM = pl.BlockSpec(memory_space=pltpu.VMEM)
SMEM = pl.BlockSpec(memory_space=pltpu.SMEM)
HBM = pl.BlockSpec(memory_space=pltpu.HBM)
MESH = pl.DeviceIdType.MESH


def remote(src, dst, send_sem, recv_sem, core, brick):
    return pltpu.make_async_remote_copy(
        src_ref=src,
        dst_ref=dst,
        send_sem=send_sem,
        recv_sem=recv_sem,
        device_id={"src": core, "brick": brick},
        device_id_type=MESH,
    )


def gather_kernel(
    bricks,
    slow_ref,
    sx_ref,
    sy_ref,
    sz_ref,
    stx_ref,
    sty_ref,
    stz_ref,
    obs_ref,
    full_ref,
    tally_ref,
    code_ref,
    spot_ref,
    table,
    line_sem,
    send_sem,
    recv_sem,
    twin_sem,
    own_sem,
    stx_buf,
    sty_buf,
    stz_buf,
    seen_buf,
    sx_buf,
    sy_buf,
    sz_buf,
    in_sem,
    word_send,
    word_recv,
):
    depth = slow_ref.shape[0]
    half = depth // 2
    lines = bricks // LOW
    me = lax.axis_index("brick")
    core = lax.axis_index("src")
    h = lax.rem(core, 2)
    twin = core + 1 - 2 * h
    line = me // LOW
    place = lax.rem(me, LOW)
    bit_x = lax.rem(me, 2)
    bit_y = lax.rem(me // 2, 2)
    flip_x = 1 - 2 * bit_x
    flip_y = 2 - 4 * bit_y
    first = me + flip_x * (1 - h) + flip_y * h
    second = me + flip_y * (1 - h) + flip_x * h
    corner = me + flip_x + flip_y
    owner = place // 2 == h
    local = lax.rem(place, 2)

    barrier = pltpu.get_barrier_semaphore()

    def greet(c, b):
        pl.semaphore_signal(barrier, inc=1, device_id={"src": c, "brick": b}, device_id_type=MESH)

    greet(twin, me)
    greet(core, first)
    greet(core, second)
    for k in range(1, lines):
        pl.when(line >= k)(lambda k=k: greet(core, me - LOW * k))
        pl.when(line + k < lines)(lambda k=k: greet(core, me + LOW * k))

    stations = [
        pltpu.make_async_copy(src, dst, in_sem.at[k])
        for k, (src, dst) in enumerate(((stx_ref, stx_buf), (sty_ref, sty_buf), (stz_ref, stz_buf)))
    ]
    spots = [
        pltpu.make_async_copy(src, dst, in_sem.at[3 + k])
        for k, (src, dst) in enumerate(((sx_ref, sx_buf), (sy_ref, sy_buf), (sz_ref, sz_buf)))
    ]
    seen_copy = pltpu.make_async_copy(obs_ref, seen_buf, in_sem.at[6])
    for load in stations:
        load.start()

    @pl.when(owner)
    def _():
        for load in spots:
            load.start()
        seen_copy.start()

    def piece(q, part):
        return full_ref.at[pl.ds(q * depth + part * half, half)]

    def copy(kind, q, brick, own=False):
        src = slow_ref.at[pl.ds(h * half, half)] if own else piece(q, h)
        return remote(src, piece(q, h), send_sem.at[kind, q], recv_sem.at[q], core, brick)

    def twin_copy(q):
        return remote(piece(q, h), piece(q, h), send_sem.at[2, q], twin_sem.at[q], twin, me)

    def along(k, up):
        dst = piece(me, h)
        src = slow_ref.at[pl.ds(h * half, half)]
        brick = me + LOW * k if up else me - LOW * k
        return remote(src, dst, line_sem.at[int(up), k], recv_sem.at[me], core, brick)

    def own_line(k, wait):
        def go(up):
            c = along(k, up)
            c.wait_send() if wait else c.start()

        pl.when(line >= k)(lambda: go(False))
        pl.when(line + k < lines)(lambda: go(True))

    def sends(q, own, wait):
        for kind, brick in ((0, first), (1, second)):
            c = copy(kind, q, brick, own)
            c.wait_send() if wait else c.start()

    own_copy = pltpu.make_async_copy(slow_ref, full_ref.at[pl.ds(me * depth, depth)], own_sem)
    seen_send = remote(obs_ref, seen_buf, word_send.at[0], word_recv.at[0], twin, me)
    spot_send = remote(spot_ref, spot_ref, word_send.at[1], word_recv.at[1], twin, me)

    def arrived(q):
        remote(piece(q, h), piece(q, h), send_sem.at[0, q], recv_sem.at[q], core, first).wait_recv()

    def on_line(base, i, act):
        pl.when((i < lines) & (line >= i))(lambda: act(base - LOW * i, -1))
        pl.when((i < lines) & (line + i < lines))(lambda: act(base + LOW * i, 1))

    def both(base, i, act):
        pl.when(i == 0)(lambda: act(base, 0))
        pl.when(i > 0)(lambda: on_line(base, i, act))

    def from_line(wait):
        def act(q, side):
            if not wait:
                arrived(q)
            sends(q, False, wait)
            c = twin_copy(q)
            c.wait_send() if wait else c.start()

        return act

    def from_first(wait):
        def act(q, side):
            if not wait:
                arrived(q)
            c = copy(1, q, second)
            c.wait_send() if wait else c.start()
            c = twin_copy(q)
            c.wait_send() if wait else c.start()

        return act

    def from_second(wait):
        def act(q, side):
            if not wait:
                arrived(q)
            c = twin_copy(q)
            c.wait_send() if wait else c.start()

        return act

    def turn(i, wait):
        on_line(me, i, from_line(wait))
        both(first, i - 1, from_first(wait))
        both(second, i - 1, from_second(wait))
        pl.when(i >= 2)(lambda: both(corner, i - 2, from_second(wait)))

    @pl.when(owner)
    def _():
        for load in spots:
            load.wait()
        sub = lax.broadcasted_iota(jnp.int32, spot_ref.shape, 0)
        spot_ref[...] = jnp.where(
            sub == 0, sx_buf[local], jnp.where(sub == 1, sy_buf[local], sz_buf[local])
        )

    for load in stations:
        load.wait()
    grid_x, cells_y, cells_z = full_ref.shape
    rows = cells_y // 8
    shift = rows.bit_length() - 1
    ring = grid_x // 2
    centre = line * (LOW * depth) + LOW * depth // 2
    sty = sty_buf[...]
    stz = stz_buf[...]
    stx = stx_buf[...]
    away = stx - centre
    away = jnp.where(away < 0, away + grid_x, away)
    upper = away < ring
    step_x = jnp.where(upper, away, grid_x - 1 - away)
    row = (step_x * rows + (sty & (rows - 1))) * 8 + (sty >> shift)
    column = jnp.where(upper, cells_z - 1 - (stz >> 1), stz >> 1)
    column = jnp.where(((stx + sty + stz) & 1) == h, column, -1)
    code_ref[0] = row
    code_ref[1] = column
    rec = row.shape[1]
    pl.semaphore_wait(barrier, lines + 2)
    pl.when(owner)(seen_send.start)
    for k in range(1, lines):
        own_line(k, False)
        if k == 1:
            sends(me, True, False)
    own_copy.start()

    hit = lax.broadcasted_iota(jnp.int32, (cells_z, rec), 0) == column

    pl.when(owner)(seen_copy.wait)
    pl.when(owner)(spot_send.start)
    pl.when(jnp.logical_not(owner))(seen_send.wait_recv)
    seen = seen_buf[pl.ds(local, 1), :] * (1.0 / spacing)
    hi = seen.astype(jnp.bfloat16).astype(jnp.float32)
    rest = seen - hi
    mid = rest.astype(jnp.bfloat16).astype(jnp.float32)
    lo = rest - mid
    for part, value in enumerate((jnp.ones_like(seen), hi, mid, lo)):
        table[pl.ds(part * cells_z, cells_z), :] = jnp.where(hit, value, 0.0).astype(jnp.bfloat16)

    tiles = TALLY // 8
    blocks = tally_ref.shape[1] // tiles

    def tally(step):
        rows_of = lax.broadcasted_iota(jnp.int32, (TALLY, rec), 0) + step * TALLY
        pick = jnp.where(rows_of == row, 1.0, 0.0).astype(jnp.bfloat16)
        got = lax.dot_general(
            pick, table[...], (((1,), (1,)), ((), ())), preferred_element_type=jnp.float32
        )
        spot = pl.ds(step * tiles, tiles)
        tally_ref[0, spot] = got[:, :cells_z].reshape(tiles, 8, cells_z)
        total = got[:, cells_z : 2 * cells_z] + (
            got[:, 2 * cells_z : 3 * cells_z] + got[:, 3 * cells_z :]
        )
        tally_ref[1, spot] = total.reshape(tiles, 8, cells_z)

    rounds = lines + 1
    tally_send = remote(
        tally_ref.at[pl.ds(0, 2)], tally_ref.at[pl.ds(2, 2)], word_send.at[2], word_recv.at[2], twin, me
    )

    @pl.loop(0, max(rounds, blocks + 1))
    def _(step):
        pl.when(step < rounds)(lambda: turn(step + 1, False))
        pl.when(step < blocks)(lambda: tally(step))
        pl.when(step == blocks)(tally_send.start)

    own_copy.wait()
    sends(me, True, True)
    for k in range(1, lines):
        own_line(k, True)

    @pl.loop(1, lines + 2)
    def _(i):
        turn(i, True)

    @pl.loop(0, bricks)
    def _(q):
        @pl.when(q != me)
        def _():
            remote(piece(q, 1 - h), piece(q, 1 - h), send_sem.at[2, q], twin_sem.at[q], twin, me).wait_recv()

    tally_send.wait()

    @pl.when(owner)
    def _():
        seen_send.wait_send()
        spot_send.wait_send()

    pl.when(jnp.logical_not(owner))(spot_send.wait_recv)


def solve_kernel(
    depth,
    cores,
    code_ref,
    spot_ref,
    full_ref,
    tally_ref,
    slots_ref,
    got_ref,
    chain,
    other,
    chain_cost,
    other_cost,
    twin_time,
    chain_weight,
    other_weight,
    chain_supply,
    other_supply,
    chain_field,
    other_field,
    packed,
    picked,
    part,
    code,
    code_sem,
    time_send,
    time_recv,
    send_sem,
    recv_sem,
    part_send,
    part_recv,
    self_sem,
):
    grid_x, cells_y, cells_z = full_ref.shape
    rows = cells_y // 8
    ring = grid_x // 2
    block = LOW * depth
    half = block // 2
    span = half + ITERS
    brick = lax.axis_index("brick")
    core = lax.axis_index("src")
    h = lax.rem(core, 2)
    twin = core + 1 - 2 * h
    group = brick // LOW
    place = lax.rem(brick, LOW)
    base = group * LOW
    peers = LOW * cores
    mine = core * LOW + place
    centre = group * block + half
    half_z = cells_z // 2

    barrier = pltpu.get_barrier_semaphore()

    def peer(k):
        t = lax.rem(mine + k, peers)
        return t // LOW, base + lax.rem(t, LOW), lax.rem(t, LOW)

    for k in range(1, peers):
        c, b, _ = peer(k)
        pl.semaphore_signal(barrier, inc=1, device_id={"src": c, "brick": b}, device_id_type=MESH)

    share = got_ref.shape[-1]
    quarter = picked.shape[0]
    load_code = pltpu.make_async_copy(code_ref.at[0], code, code_sem)
    load_code.start()

    lane = lax.broadcasted_iota(jnp.int32, (8, cells_z), 1)
    sub = lax.broadcasted_iota(jnp.int32, (8, cells_z), 0)
    sub_first = sub == 0
    sub_last = sub == 7
    upper = lane >= half_z
    inner = jnp.where(upper, cells_z - 1 - lane, lane)
    parity = [lax.rem(q + h, 2) for q in range(2)]
    cell_z = [inner * 2 + jnp.where(upper, 1 - p, p) for p in parity]
    from_low = [(lane & 1) == p for p in parity]
    edge_z = [(lane & (half_z - 1)) == p * (half_z - 1) for p in parity]
    slide = [1 + p * (cells_z - 2) for p in parity]
    mirror = cells_z - 1 - lane

    def slot(i, v):
        return (i + 1) * rows + v

    sx = spot_ref[0:1, :]
    sy = spot_ref[1:2, :]
    sz = spot_ref[2:3, :]
    unit = (start_slowness * spacing) ** 2
    flat = []
    for q in range(2):
        dz = (cell_z[q] - sz).astype(jnp.float32)
        dz = dz * dz
        for v in range(rows):
            dy = (sub * rows + v - sy).astype(jnp.float32)
            flat.append((dy * dy + dz) * unit)

    @pl.loop(0, ring // 2)
    def _(pair):
        for j in range(2):
            i = pair * 2 + j
            x_low = centre - 1 - i
            x_low = jnp.where(x_low < 0, x_low + grid_x, x_low)
            x_high = centre + i
            x_high = jnp.where(x_high >= grid_x, x_high - grid_x, x_high)
            dx = (jnp.where(upper, x_high, x_low) - sx).astype(jnp.float32)
            dx = dx * dx * unit
            for v in range(rows):
                q = (j + 1 + v) % 2
                low = full_ref[x_low, pl.ds(v, 8, stride=rows), :]
                high = full_ref[x_high, pl.ds(v, 8, stride=rows), :]
                pair_of = (
                    (chain, chain_cost, q, jnp.where(from_low[q], low, high)),
                    (other, other_cost, 1 - q, jnp.where(from_low[q], high, low)),
                )
                for field, cost, k, natural in pair_of if q else pair_of[::-1]:
                    slow = jnp.take_along_axis(natural, cell_z[k], axis=1)
                    square = dx + flat[k * rows + v]
                    start = square * lax.rsqrt(jnp.maximum(square, unit * 0.5))
                    cost[i * rows + v] = (2.0 * half_step) * slow
                    field[slot(i, v)] = start + half_step * slow

    cuts = {
        b: jnp.where(upper, grid_x - centre, centre) == b for b in range(half, ring, half) if (b // half) % 2
    }

    def swing(one):
        return jnp.take_along_axis(one, mirror, axis=1)

    def across_z(one, k):
        return pltpu.roll(one, slide[k], 1)

    def y_up(cur, v):
        return cur[v + 1] if v + 1 < rows else pltpu.roll(cur[0], 7, 0)

    def y_down(cur, v):
        return cur[v - 1] if v else pltpu.roll(cur[rows - 1], 1, 0)

    def order(i):
        return [v ^ (i & 1) for v in range(rows)]

    def sweep(dst, cost, src, turned):
        for i in range(ring):
            cur = [src[slot(i, v)] for v in range(rows)]
            if i == 0 or i + 1 == ring:
                swung = [swing(one) for one in cur]
            for v in order(i + turned):
                q = (i + 1 + v) % 2
                before = src[slot(i - 1, v)] if i else swung[v]
                after = src[slot(i + 1, v)] if i + 1 < ring else swung[v]
                if i in cuts:
                    before = jnp.where(cuts[i], big_value, before)
                if i + 1 in cuts:
                    after = jnp.where(cuts[i + 1], big_value, after)
                up = y_up(cur, v)
                down = y_down(cur, v)
                if v + 1 == rows:
                    up = jnp.where(sub_last, big_value, up)
                if v == 0:
                    down = jnp.where(sub_first, big_value, down)
                k = q ^ turned
                across = jnp.where(edge_z[k], cur[v], across_z(cur[v], k))
                low = jnp.minimum(
                    jnp.minimum(jnp.minimum(before, after), jnp.minimum(up, down)),
                    jnp.minimum(cur[v], across),
                )
                dst[slot(i, v)] = jnp.minimum(dst[slot(i, v)], low + cost[i * rows + v])

    assert ITERS % 2 == 0

    @pl.loop(0, ITERS // 2)
    def _(_step):
        sweep(other, other_cost, chain, 1)
        sweep(chain, chain_cost, other, 0)

    @pl.loop(0, ring)
    def _(i):
        for v in range(rows):
            chain[slot(i, v)] = (chain[slot(i, v)] - 0.5 * chain_cost[i * rows + v]) * (1.0 / spacing)

    for v in range(rows):
        chain[slot(-1, v)] = swing(chain[slot(0, v)])

    pl.semaphore_wait(barrier, peers - 1)
    reach = span + 2
    time_copy = remote(
        chain.at[pl.ds(0, reach * rows)], twin_time, time_send, time_recv, twin, brick
    )
    time_copy.start()

    load_code.wait()
    unroll = 16

    @pl.loop(0, quarter // unroll)
    def _(n):
        for j in range(unroll):
            r = n * unroll + j
            at = code[0, group * quarter + r]
            picked[pl.ds(r, 1), :] = chain[(at >> 3) + rows, pl.ds(at & 7, 1), :]

    column = code_ref[1, :, pl.ds(pl.multiple_of(group * quarter, 128), quarter)]
    turned = jnp.transpose(picked[...])
    here = lax.broadcasted_iota(jnp.int32, turned.shape, 0) == column
    arrived = jnp.sum(jnp.where(here, turned, 0.0), axis=0, keepdims=True) * spacing
    for k in range(LOW):
        part[k] = arrived[:, k * share : (k + 1) * share]

    for v in range(rows):
        chain_field[slot(span - 2, v)] = jnp.zeros((8, cells_z), jnp.float32)
        chain_field[slot(span - 1, v)] = jnp.zeros((8, cells_z), jnp.float32)
        chain_field[slot(span, v)] = jnp.zeros((8, cells_z), jnp.float32)
        other_field[slot(span, v)] = jnp.zeros((8, cells_z), jnp.float32)

    time_copy.wait_recv()
    bound = jnp.where(upper, grid_x - centre, centre)

    def weigh(at, i, own, theirs, weight, supply, field, tally, turned):
        cur = [theirs[slot(at, v)] for v in range(rows)]
        cut_before = bound == at
        cut_after = bound == at + 1
        for v in order(i + turned):
            q = (i + 1 + v) % 2
            one = own[slot(at, v)]

            def gain(value):
                return jnp.maximum(value - one, 0.0)

            before = gain(theirs[slot(at - 1, v)])
            after = gain(theirs[slot(at + 1, v)])
            if i % half == 0:
                before = jnp.where(cut_before, 0.0, before)
            if (i + 1) % half == 0:
                after = jnp.where(cut_after, 0.0, after)
            up = gain(y_up(cur, v))
            down = gain(y_down(cur, v))
            if v + 1 == rows:
                up = jnp.where(sub_last, 0.0, up)
            if v == 0:
                down = jnp.where(sub_first, 0.0, down)
            k = q ^ turned
            across = jnp.where(edge_z[k], 0.0, gain(across_z(cur[v], k)))
            parts = (before, after, down, up, gain(cur[v]), across)
            total = ((parts[0] + parts[1]) + (parts[2] + parts[3])) + (parts[4] + parts[5])
            inverse = 1.0 / (1.0 + total)
            spot = at * rows + v
            for n, gained in enumerate(parts):
                weight[n, spot] = gained * inverse
            value = (tally_ref[tally, spot] * one - tally_ref[tally + 1, spot]) * inverse
            supply[spot] = value
            if turned:
                field[slot(at, v)] = value

    @pl.loop(0, span // half)
    def _(chunk):
        for i in range(half):
            at = chunk * half + i
            weigh(at, i, twin_time, chain, other_weight, other_supply, other_field, 2, 1)
            weigh(at, i, chain, twin_time, chain_weight, chain_supply, chain_field, 0, 0)

    for v in range(rows):
        other_field[slot(-1, v)] = swing(other_field[slot(0, v)])

    def backward(count, dst, weight, supply, src, turned):
        for i in range(count):
            cur = [src[slot(i, v)] for v in range(rows)]
            if i == 0:
                swung = [swing(one) for one in cur]
            for v in order(i + turned):
                q = (i + 1 + v) % 2
                spot = i * rows + v
                before = src[slot(i - 1, v)] if i else swung[v]
                acc = supply[spot] + weight[0, spot] * before
                acc = acc + weight[1, spot] * src[slot(i + 1, v)]
                side = weight[2, spot] * y_down(cur, v) + weight[3, spot] * y_up(cur, v)
                across = across_z(cur[v], q ^ turned)
                acc = (acc + side) + (weight[4, spot] * cur[v] + weight[5, spot] * across)
                dst[slot(i, v)] = acc

    def rounds(first, times):
        count = half + ITERS - first

        @pl.loop(0, times)
        def _(_step):
            backward(count, chain_field, chain_weight, chain_supply, other_field, 0)
            backward(count - 1, other_field, other_weight, other_supply, chain_field, 1)

    rounds(2, 3)
    rounds(8, 2)
    rounds(12, 2)
    backward(half, chain_field, chain_weight, chain_supply, other_field, 0)

    for k in range(LOW):
        for t in range(0, depth, 2):
            low_side = k < LOW // 2
            near, next_to = (
                (half - 1 - (k * depth + t + n)) if low_side else (k * depth + t + n - half) for n in range(2)
            )
            for v in range(rows):
                a = chain_field[slot(near, v)]
                b = chain_field[slot(next_to, v)]
                both = jnp.where(upper, swing(b), a) if low_side else jnp.where(upper, b, swing(a))
                packed[k, t // 2, pl.ds(v, 8, stride=rows), :] = both

    keep = slots_ref.shape[2]

    def ship(k):
        c, b, p = peer(k)
        return remote(
            packed.at[p, :, pl.ds(c * keep, keep)], slots_ref.at[mine], send_sem.at[k], recv_sem.at[mine], c, b
        )

    for k in range(1, peers):
        ship(k).start()
    stay = pltpu.make_async_copy(
        packed.at[place, :, pl.ds(core * keep, keep)], slots_ref.at[mine], self_sem
    )
    stay.start()

    target = core - h + place // 2
    local = lax.rem(place, 2)

    def word(k):
        return remote(
            part.at[k], got_ref.at[local, h], part_send.at[k], part_recv.at[local, h], target, base + k
        )

    def home(k):
        return (target == core) & (place == k)

    for k in range(LOW):
        pl.when(jnp.logical_not(home(k)))(word(k).start)

        @pl.when(home(k))
        def _():
            got_ref[local, h] = part[k]

    def word_in(n, side):
        return remote(
            part.at[0], got_ref.at[n, side], part_send.at[0], part_recv.at[n, side], core, brick
        )

    for n in range(2):
        for side in range(2):
            from_me = (place == 2 * h + n) & (h == side)
            pl.when(jnp.logical_not(from_me))(word_in(n, side).wait_recv)
    for k in range(1, peers):
        m = lax.rem(mine + k, peers)
        remote(
            packed.at[0, :, pl.ds(0, keep)], slots_ref.at[m], send_sem.at[k], recv_sem.at[m], core, brick
        ).wait_recv()
    for k in range(1, peers):
        ship(k).wait_send()
    for k in range(LOW):
        pl.when(jnp.logical_not(home(k)))(word(k).wait_send)
    stay.wait()
    time_copy.wait_send()


def finish_kernel(cores, slots_ref, got_ref, full_ref, out_ref, arr_ref):
    depth, keep, cells_z = out_ref.shape
    half_z = cells_z // 2
    first = lax.axis_index("brick") * depth
    row = pl.multiple_of(lax.axis_index("src") * keep, 8)
    lane = lax.broadcasted_iota(jnp.int32, (8, cells_z), 1)
    sub = lax.broadcasted_iota(jnp.int32, (8, cells_z), 0)
    upper = lane >= half_z
    plain = ((sub + jnp.where(upper, 1, 0)) & 1) == 0
    join = jnp.where((lane & 1) == 0, lane >> 1, cells_z - 1 - (lane >> 1))
    mirror = cells_z - 1 - lane
    for t in range(depth // 2):
        for y in range(0, keep, 8):
            sums = []
            for colour in range(2):
                total = None
                for c in range(colour, cores, 2):
                    for k in range(LOW):
                        one = slots_ref[c * LOW + k, t, pl.ds(y, 8), :]
                        total = one if total is None else total + one
                sums.append(total)
            even = jnp.where(plain, sums[0], sums[1])
            odd = jnp.where(plain, sums[1], sums[0])
            moved = jnp.take_along_axis(jnp.where(upper, even, odd), mirror, axis=1)
            for n, packed in enumerate((jnp.where(upper, moved, even), jnp.where(upper, odd, moved))):
                value = jnp.take_along_axis(packed, join, axis=1)
                slow = full_ref[first + 2 * t + n, pl.ds(row + y, 8), :]
                out_ref[2 * t + n, pl.ds(y, 8), :] = (slow * spacing) * value
    for n in range(2):
        arr_ref[pl.ds(n, 1), :] = got_ref[n, 0] + got_ref[n, 1]


def per_device(slowness, source_x, source_y, source_z, station_x, station_y, station_z, observed):
    bricks = lax.axis_size("brick")
    cores = lax.axis_size("src")
    depth, cells_y, cells_z = slowness.shape
    grid_x = depth * bricks
    rec = station_x.shape[0]
    rows = cells_y // 8
    ring = grid_x // 2
    half = LOW * depth // 2
    span = half + ITERS
    assert source_x.shape[0] == 2 and bricks % LOW == 0 and cores % 2 == 0
    assert half % 2 == 0 and span % half == 0 and span + 1 <= ring and (span * rows * 8) % TALLY == 0
    f32 = jnp.float32
    i32 = jnp.int32

    full, tally, code, spot = pl.pallas_call(
        functools.partial(gather_kernel, bricks),
        name="gather",
        out_shape=(
            jax.ShapeDtypeStruct((grid_x, cells_y, cells_z), f32),
            jax.ShapeDtypeStruct((4, span * rows, 8, cells_z), f32),
            jax.ShapeDtypeStruct((2, 1, rec), i32),
            jax.ShapeDtypeStruct((8, cells_z), i32),
        ),
        in_specs=[HBM] * 8,
        out_specs=(VMEM, VMEM, VMEM, VMEM),
        scratch_shapes=[
            pltpu.VMEM((4 * cells_z, rec), jnp.bfloat16),
            pltpu.SemaphoreType.DMA((2, bricks // LOW)),
            pltpu.SemaphoreType.DMA((3, bricks)),
            pltpu.SemaphoreType.DMA((bricks,)),
            pltpu.SemaphoreType.DMA((bricks,)),
            pltpu.SemaphoreType.DMA,
            pltpu.VMEM((1, rec), i32),
            pltpu.VMEM((1, rec), i32),
            pltpu.VMEM((1, rec), i32),
            pltpu.VMEM(observed.shape, f32),
            pltpu.SMEM((2,), i32),
            pltpu.SMEM((2,), i32),
            pltpu.SMEM((2,), i32),
            pltpu.SemaphoreType.DMA((7,)),
            pltpu.SemaphoreType.DMA((3,)),
            pltpu.SemaphoreType.DMA((3,)),
        ],
        compiler_params=pltpu.CompilerParams(
            collective_id=0, has_side_effects=True, vmem_limit_bytes=GATHER_VMEM
        ),
    )(
        *(
            pltpu.with_memory_space_constraint(a, pltpu.HBM)
            for a in (
                slowness,
                source_x,
                source_y,
                source_z,
                station_x[None],
                station_y[None],
                station_z[None],
                observed,
            )
        )
    )

    share = rec // bricks
    quarter = share * LOW
    keep = cells_y // cores
    layer = (rows, 8, cells_z)
    ring_shape = ((ring + 2) * rows, 8, cells_z)
    slots, got = pl.pallas_call(
        functools.partial(solve_kernel, depth, cores),
        name="solve",
        out_shape=(
            jax.ShapeDtypeStruct((LOW * cores, depth // 2, keep, cells_z), f32),
            jax.ShapeDtypeStruct((2, 2, 1, share), f32),
        ),
        in_specs=[VMEM] * 4,
        out_specs=(VMEM, VMEM),
        scratch_shapes=[
            pltpu.VMEM(ring_shape, f32),
            pltpu.VMEM(ring_shape, f32),
            pltpu.VMEM((ring * rows, 8, cells_z), f32),
            pltpu.VMEM((ring * rows, 8, cells_z), f32),
            pltpu.VMEM(((span + 2) * rows, 8, cells_z), f32),
            pltpu.VMEM((6, span * rows, 8, cells_z), f32),
            pltpu.VMEM((6, span * rows, 8, cells_z), f32),
            pltpu.VMEM((span * rows, 8, cells_z), f32),
            pltpu.VMEM((span * rows, 8, cells_z), f32),
            pltpu.VMEM(((span + 2) * rows, 8, cells_z), f32),
            pltpu.VMEM(((span + 2) * rows, 8, cells_z), f32),
            pltpu.VMEM((LOW, depth // 2, cells_y, cells_z), f32),
            pltpu.VMEM((quarter, cells_z), f32),
            pltpu.VMEM((LOW, 1, share), f32),
            pltpu.SMEM((1, rec), i32),
            pltpu.SemaphoreType.DMA,
            pltpu.SemaphoreType.DMA,
            pltpu.SemaphoreType.DMA,
            pltpu.SemaphoreType.DMA((LOW * cores,)),
            pltpu.SemaphoreType.DMA((LOW * cores,)),
            pltpu.SemaphoreType.DMA((LOW,)),
            pltpu.SemaphoreType.DMA((2, 2)),
            pltpu.SemaphoreType.DMA,
        ],
        compiler_params=pltpu.CompilerParams(
            collective_id=1, has_side_effects=True, vmem_limit_bytes=SOLVE_VMEM
        ),
    )(code, spot, full, tally)

    return tuple(
        pl.pallas_call(
            functools.partial(finish_kernel, cores),
            name="finish",
            out_shape=(
                jax.ShapeDtypeStruct((depth, keep, cells_z), f32),
                jax.ShapeDtypeStruct((2, share), f32),
            ),
            in_specs=[VMEM] * 3,
            compiler_params=pltpu.CompilerParams(vmem_limit_bytes=FINISH_VMEM),
        )(slots, got, full)
    )


def solution(mesh):
    in_specs = (P("brick", None, None), P("src"), P("src"), P("src"), P(), P(), P(), P("src", None))
    out_specs = (P("brick", "src", None), P("src", "brick"))
    return jax.shard_map(
        per_device, mesh=mesh, in_specs=in_specs, out_specs=out_specs, check_vma=False
    )
```

```python
import functools

import jax
import jax.numpy as jnp
from jax import lax
from jax.experimental import pallas as pl
from jax.experimental.pallas import tpu as pltpu
from jax.sharding import PartitionSpec as P

ITERS = 16

spacing = 0.015625
big_value = 1000000.0
start_slowness = 2.0
half_step = 0.5 * spacing
LOW = 4
GATHER_VMEM = 24 << 20
SOLVE_VMEM = 44 << 20
FINISH_VMEM = 8 << 20
TALLY = 512

VMEM = pl.BlockSpec(memory_space=pltpu.VMEM)
SMEM = pl.BlockSpec(memory_space=pltpu.SMEM)
HBM = pl.BlockSpec(memory_space=pltpu.HBM)
MESH = pl.DeviceIdType.MESH


def remote(src, dst, send_sem, recv_sem, core, brick):
    return pltpu.make_async_remote_copy(
        src_ref=src,
        dst_ref=dst,
        send_sem=send_sem,
        recv_sem=recv_sem,
        device_id={"src": core, "brick": brick},
        device_id_type=MESH,
    )


def gather_kernel(
    bricks,
    slow_ref,
    sx_ref,
    sy_ref,
    sz_ref,
    stx_ref,
    sty_ref,
    stz_ref,
    obs_ref,
    full_ref,
    tally_ref,
    code_ref,
    spot_ref,
    table,
    line_sem,
    send_sem,
    recv_sem,
    twin_sem,
    own_sem,
    stx_buf,
    sty_buf,
    stz_buf,
    seen_buf,
    sx_buf,
    sy_buf,
    sz_buf,
    in_sem,
    word_send,
    word_recv,
):
    depth = slow_ref.shape[0]
    half = depth // 2
    lines = bricks // LOW
    me = lax.axis_index("brick")
    core = lax.axis_index("src")
    h = lax.rem(core, 2)
    twin = core + 1 - 2 * h
    line = me // LOW
    place = lax.rem(me, LOW)
    bit_x = lax.rem(me, 2)
    bit_y = lax.rem(me // 2, 2)
    flip_x = 1 - 2 * bit_x
    flip_y = 2 - 4 * bit_y
    first = me + flip_x * (1 - h) + flip_y * h
    second = me + flip_y * (1 - h) + flip_x * h
    corner = me + flip_x + flip_y
    owner = place // 2 == h
    local = lax.rem(place, 2)

    barrier = pltpu.get_barrier_semaphore()

    def greet(c, b):
        pl.semaphore_signal(barrier, inc=1, device_id={"src": c, "brick": b}, device_id_type=MESH)

    greet(twin, me)
    greet(core, first)
    greet(core, second)
    for k in range(1, lines):
        pl.when(line >= k)(lambda k=k: greet(core, me - LOW * k))
        pl.when(line + k < lines)(lambda k=k: greet(core, me + LOW * k))

    stations = [
        pltpu.make_async_copy(src, dst, in_sem.at[k])
        for k, (src, dst) in enumerate(((stx_ref, stx_buf), (sty_ref, sty_buf), (stz_ref, stz_buf)))
    ]
    spots = [
        pltpu.make_async_copy(src, dst, in_sem.at[3 + k])
        for k, (src, dst) in enumerate(((sx_ref, sx_buf), (sy_ref, sy_buf), (sz_ref, sz_buf)))
    ]
    seen_copy = pltpu.make_async_copy(obs_ref, seen_buf, in_sem.at[6])
    for load in stations:
        load.start()

    @pl.when(owner)
    def _():
        for load in spots:
            load.start()
        seen_copy.start()

    def piece(q, part):
        return full_ref.at[pl.ds(q * depth + part * half, half)]

    def copy(kind, q, brick, own=False):
        src = slow_ref.at[pl.ds(h * half, half)] if own else piece(q, h)
        return remote(src, piece(q, h), send_sem.at[kind, q], recv_sem.at[q], core, brick)

    def twin_copy(q):
        return remote(piece(q, h), piece(q, h), send_sem.at[2, q], twin_sem.at[q], twin, me)

    def along(k, up):
        dst = piece(me, h)
        src = slow_ref.at[pl.ds(h * half, half)]
        brick = me + LOW * k if up else me - LOW * k
        return remote(src, dst, line_sem.at[int(up), k], recv_sem.at[me], core, brick)

    def own_line(k, wait):
        def go(up):
            c = along(k, up)
            c.wait_send() if wait else c.start()

        pl.when(line >= k)(lambda: go(False))
        pl.when(line + k < lines)(lambda: go(True))

    def sends(q, own, wait):
        for kind, brick in ((0, first), (1, second)):
            c = copy(kind, q, brick, own)
            c.wait_send() if wait else c.start()

    own_copy = pltpu.make_async_copy(slow_ref, full_ref.at[pl.ds(me * depth, depth)], own_sem)
    seen_send = remote(obs_ref, seen_buf, word_send.at[0], word_recv.at[0], twin, me)
    spot_send = remote(spot_ref, spot_ref, word_send.at[1], word_recv.at[1], twin, me)

    pl.semaphore_wait(barrier, lines + 2)
    pl.when(owner)(seen_send.start)
    for k in range(1, lines):
        own_line(k, False)
        if k == 1:
            sends(me, True, False)
    own_copy.start()

    def arrived(q):
        remote(piece(q, h), piece(q, h), send_sem.at[0, q], recv_sem.at[q], core, first).wait_recv()

    def on_line(base, i, act):
        pl.when((i < lines) & (line >= i))(lambda: act(base - LOW * i, -1))
        pl.when((i < lines) & (line + i < lines))(lambda: act(base + LOW * i, 1))

    def both(base, i, act):
        pl.when(i == 0)(lambda: act(base, 0))
        pl.when(i > 0)(lambda: on_line(base, i, act))

    def from_line(wait):
        def act(q, side):
            if not wait:
                arrived(q)
            sends(q, False, wait)
            c = twin_copy(q)
            c.wait_send() if wait else c.start()

        return act

    def from_first(wait):
        def act(q, side):
            if not wait:
                arrived(q)
            c = copy(1, q, second)
            c.wait_send() if wait else c.start()
            c = twin_copy(q)
            c.wait_send() if wait else c.start()

        return act

    def from_second(wait):
        def act(q, side):
            if not wait:
                arrived(q)
            c = twin_copy(q)
            c.wait_send() if wait else c.start()

        return act

    def turn(i, wait):
        on_line(me, i, from_line(wait))
        both(first, i - 1, from_first(wait))
        both(second, i - 1, from_second(wait))
        pl.when(i >= 2)(lambda: both(corner, i - 2, from_second(wait)))

    @pl.when(owner)
    def _():
        for load in spots:
            load.wait()
        sub = lax.broadcasted_iota(jnp.int32, spot_ref.shape, 0)
        spot_ref[...] = jnp.where(
            sub == 0, sx_buf[local], jnp.where(sub == 1, sy_buf[local], sz_buf[local])
        )

    for load in stations:
        load.wait()
    grid_x, cells_y, cells_z = full_ref.shape
    rows = cells_y // 8
    shift = rows.bit_length() - 1
    ring = grid_x // 2
    centre = line * (LOW * depth) + LOW * depth // 2
    sty = sty_buf[...]
    stz = stz_buf[...]
    stx = stx_buf[...]
    away = stx - centre
    away = jnp.where(away < 0, away + grid_x, away)
    upper = away < ring
    step_x = jnp.where(upper, away, grid_x - 1 - away)
    row = (step_x * rows + (sty & (rows - 1))) * 8 + (sty >> shift)
    column = jnp.where(upper, cells_z - 1 - (stz >> 1), stz >> 1)
    column = jnp.where(((stx + sty + stz) & 1) == h, column, -1)
    code_ref[0] = row
    code_ref[1] = column
    rec = row.shape[1]
    hit = lax.broadcasted_iota(jnp.int32, (cells_z, rec), 0) == column

    pl.when(owner)(seen_copy.wait)
    pl.when(owner)(spot_send.start)
    pl.when(jnp.logical_not(owner))(seen_send.wait_recv)
    seen = seen_buf[pl.ds(local, 1), :] * (1.0 / spacing)
    hi = seen.astype(jnp.bfloat16).astype(jnp.float32)
    rest = seen - hi
    mid = rest.astype(jnp.bfloat16).astype(jnp.float32)
    lo = rest - mid
    for part, value in enumerate((jnp.ones_like(seen), hi, mid, lo)):
        table[pl.ds(part * cells_z, cells_z), :] = jnp.where(hit, value, 0.0).astype(jnp.bfloat16)

    tiles = TALLY // 8
    blocks = tally_ref.shape[1] // tiles

    def tally(step):
        rows_of = lax.broadcasted_iota(jnp.int32, (TALLY, rec), 0) + step * TALLY
        pick = jnp.where(rows_of == row, 1.0, 0.0).astype(jnp.bfloat16)
        got = lax.dot_general(
            pick, table[...], (((1,), (1,)), ((), ())), preferred_element_type=jnp.float32
        )
        spot = pl.ds(step * tiles, tiles)
        tally_ref[0, spot] = got[:, :cells_z].reshape(tiles, 8, cells_z)
        total = got[:, cells_z : 2 * cells_z] + (
            got[:, 2 * cells_z : 3 * cells_z] + got[:, 3 * cells_z :]
        )
        tally_ref[1, spot] = total.reshape(tiles, 8, cells_z)

    rounds = lines + 1
    tally_send = remote(
        tally_ref.at[pl.ds(0, 2)], tally_ref.at[pl.ds(2, 2)], word_send.at[2], word_recv.at[2], twin, me
    )

    @pl.loop(0, max(rounds, blocks + 1))
    def _(step):
        pl.when(step < rounds)(lambda: turn(step + 1, False))
        pl.when(step < blocks)(lambda: tally(step))
        pl.when(step == blocks)(tally_send.start)

    own_copy.wait()
    sends(me, True, True)
    for k in range(1, lines):
        own_line(k, True)

    @pl.loop(1, lines + 2)
    def _(i):
        turn(i, True)

    @pl.loop(0, bricks)
    def _(q):
        @pl.when(q != me)
        def _():
            remote(piece(q, 1 - h), piece(q, 1 - h), send_sem.at[2, q], twin_sem.at[q], twin, me).wait_recv()

    tally_send.wait()

    @pl.when(owner)
    def _():
        seen_send.wait_send()
        spot_send.wait_send()

    pl.when(jnp.logical_not(owner))(spot_send.wait_recv)


def solve_kernel(
    depth,
    cores,
    code_ref,
    spot_ref,
    full_ref,
    tally_ref,
    slots_ref,
    got_ref,
    chain,
    other,
    chain_cost,
    other_cost,
    twin_time,
    chain_weight,
    other_weight,
    chain_supply,
    other_supply,
    chain_field,
    other_field,
    packed,
    picked,
    part,
    code,
    code_sem,
    time_send,
    time_recv,
    send_sem,
    recv_sem,
    part_send,
    part_recv,
    self_sem,
):
    grid_x, cells_y, cells_z = full_ref.shape
    rows = cells_y // 8
    ring = grid_x // 2
    block = LOW * depth
    half = block // 2
    span = half + ITERS
    brick = lax.axis_index("brick")
    core = lax.axis_index("src")
    h = lax.rem(core, 2)
    twin = core + 1 - 2 * h
    group = brick // LOW
    place = lax.rem(brick, LOW)
    base = group * LOW
    peers = LOW * cores
    mine = core * LOW + place
    centre = group * block + half
    half_z = cells_z // 2

    barrier = pltpu.get_barrier_semaphore()

    def peer(k):
        t = lax.rem(mine + k, peers)
        return t // LOW, base + lax.rem(t, LOW), lax.rem(t, LOW)

    for k in range(1, peers):
        c, b, _ = peer(k)
        pl.semaphore_signal(barrier, inc=1, device_id={"src": c, "brick": b}, device_id_type=MESH)

    share = got_ref.shape[-1]
    quarter = picked.shape[0]
    load_code = pltpu.make_async_copy(code_ref.at[0], code, code_sem)
    load_code.start()

    lane = lax.broadcasted_iota(jnp.int32, (8, cells_z), 1)
    sub = lax.broadcasted_iota(jnp.int32, (8, cells_z), 0)
    sub_first = sub == 0
    sub_last = sub == 7
    upper = lane >= half_z
    inner = jnp.where(upper, cells_z - 1 - lane, lane)
    parity = [lax.rem(q + h, 2) for q in range(2)]
    cell_z = [inner * 2 + jnp.where(upper, 1 - p, p) for p in parity]
    from_low = [(lane & 1) == p for p in parity]
    edge_z = [(lane & (half_z - 1)) == p * (half_z - 1) for p in parity]
    slide = [1 + p * (cells_z - 2) for p in parity]
    mirror = cells_z - 1 - lane

    def slot(i, v):
        return (i + 1) * rows + v

    sx = spot_ref[0:1, :]
    sy = spot_ref[1:2, :]
    sz = spot_ref[2:3, :]
    unit = (start_slowness * spacing) ** 2
    flat = []
    for q in range(2):
        dz = (cell_z[q] - sz).astype(jnp.float32)
        dz = dz * dz
        for v in range(rows):
            dy = (sub * rows + v - sy).astype(jnp.float32)
            flat.append((dy * dy + dz) * unit)

    @pl.loop(0, ring // 4)
    def _(quad):
        for j in range(4):
            i = quad * 4 + j
            x_low = centre - 1 - i
            x_low = jnp.where(x_low < 0, x_low + grid_x, x_low)
            x_high = centre + i
            x_high = jnp.where(x_high >= grid_x, x_high - grid_x, x_high)
            dx = (jnp.where(upper, x_high, x_low) - sx).astype(jnp.float32)
            dx = dx * dx * unit
            for v in range(rows):
                q = (j + 1 + v) % 2
                low = full_ref[x_low, pl.ds(v, 8, stride=rows), :]
                high = full_ref[x_high, pl.ds(v, 8, stride=rows), :]
                pair_of = (
                    (chain, chain_cost, q, jnp.where(from_low[q], low, high)),
                    (other, other_cost, 1 - q, jnp.where(from_low[q], high, low)),
                )
                for field, cost, k, natural in pair_of if q else pair_of[::-1]:
                    slow = jnp.take_along_axis(natural, cell_z[k], axis=1)
                    square = dx + flat[k * rows + v]
                    start = square * lax.rsqrt(jnp.maximum(square, unit * 0.5))
                    cost[i * rows + v] = (2.0 * half_step) * slow
                    field[slot(i, v)] = start + half_step * slow

    cuts = {
        b: jnp.where(upper, grid_x - centre, centre) == b for b in range(half, ring, half) if (b // half) % 2
    }

    def swing(one):
        return jnp.take_along_axis(one, mirror, axis=1)

    def across_z(one, k):
        return pltpu.roll(one, slide[k], 1)

    def y_up(cur, v):
        return cur[v + 1] if v + 1 < rows else pltpu.roll(cur[0], 7, 0)

    def y_down(cur, v):
        return cur[v - 1] if v else pltpu.roll(cur[rows - 1], 1, 0)

    def layer_of(ref, i):
        return [ref[slot(i, v)] for v in range(rows)]

    def sweep(dst, cost, src, turned):
        cur = layer_of(src, 0)
        prev = [swing(one) for one in cur]
        for i in range(ring):
            after_of = layer_of(src, i + 1) if i + 1 < ring else [swing(one) for one in cur]
            for v in range(rows):
                q = (i + 1 + v) % 2
                before = prev[v]
                after = after_of[v]
                if i in cuts:
                    before = jnp.where(cuts[i], big_value, before)
                if i + 1 in cuts:
                    after = jnp.where(cuts[i + 1], big_value, after)
                up = y_up(cur, v)
                down = y_down(cur, v)
                if v + 1 == rows:
                    up = jnp.where(sub_last, big_value, up)
                if v == 0:
                    down = jnp.where(sub_first, big_value, down)
                k = q ^ turned
                across = jnp.where(edge_z[k], cur[v], across_z(cur[v], k))
                low = jnp.minimum(across, cur[v])
                for value in (before, after, down, up):
                    low = jnp.minimum(low, value)
                dst[slot(i, v)] = jnp.minimum(dst[slot(i, v)], low + cost[i * rows + v])
            prev, cur = cur, after_of

    assert ITERS % 2 == 0

    @pl.loop(0, ITERS // 2)
    def _(_step):
        sweep(other, other_cost, chain, 1)
        sweep(chain, chain_cost, other, 0)

    @pl.loop(0, ring)
    def _(i):
        for v in range(rows):
            chain[slot(i, v)] = (chain[slot(i, v)] - 0.5 * chain_cost[i * rows + v]) * (1.0 / spacing)

    for v in range(rows):
        chain[slot(-1, v)] = swing(chain[slot(0, v)])

    pl.semaphore_wait(barrier, peers - 1)
    stops = [0] + [(2 + n * half) * rows for n in range(1, span // half + 1)]
    time_copies = []
    for n, (low, high) in enumerate(zip(stops, stops[1:])):
        part_of = pl.ds(low, high - low)
        time_copies.append(
            remote(chain.at[part_of], twin_time.at[part_of], time_send.at[n], time_recv.at[n], twin, brick)
        )
    for copy in time_copies:
        copy.start()

    load_code.wait()
    unroll = 16

    @pl.loop(0, quarter // unroll)
    def _(n):
        for j in range(unroll):
            r = n * unroll + j
            at = code[0, group * quarter + r]
            picked[pl.ds(r, 1), :] = chain[(at >> 3) + rows, pl.ds(at & 7, 1), :]

    column = code_ref[1, :, pl.ds(pl.multiple_of(group * quarter, 128), quarter)]
    turned = jnp.transpose(picked[...])
    here = lax.broadcasted_iota(jnp.int32, turned.shape, 0) == column
    arrived = jnp.sum(jnp.where(here, turned, 0.0), axis=0, keepdims=True) * spacing
    for k in range(LOW):
        part[k] = arrived[:, k * share : (k + 1) * share]

    for v in range(rows):
        chain_field[slot(span - 2, v)] = jnp.zeros((8, cells_z), jnp.float32)
        chain_field[slot(span - 1, v)] = jnp.zeros((8, cells_z), jnp.float32)
        chain_field[slot(span, v)] = jnp.zeros((8, cells_z), jnp.float32)
        other_field[slot(span, v)] = jnp.zeros((8, cells_z), jnp.float32)

    bound = jnp.where(upper, grid_x - centre, centre)

    def weigh(at, i, own, theirs, weight, supply, field, tally, turned):
        cur = [theirs[slot(at, v)] for v in range(rows)]
        cut_before = bound == at
        cut_after = bound == at + 1
        for v in range(rows):
            q = (i + 1 + v) % 2
            one = own[slot(at, v)]

            def gain(value):
                return jnp.maximum(value - one, 0.0)

            before = gain(theirs[slot(at - 1, v)])
            after = gain(theirs[slot(at + 1, v)])
            if i % half == 0:
                before = jnp.where(cut_before, 0.0, before)
            if (i + 1) % half == 0:
                after = jnp.where(cut_after, 0.0, after)
            up = gain(y_up(cur, v))
            down = gain(y_down(cur, v))
            if v + 1 == rows:
                up = jnp.where(sub_last, 0.0, up)
            if v == 0:
                down = jnp.where(sub_first, 0.0, down)
            k = q ^ turned
            across = jnp.where(edge_z[k], 0.0, gain(across_z(cur[v], k)))
            parts = (before, after, down, up, gain(cur[v]), across)
            total = ((parts[0] + parts[1]) + (parts[2] + parts[3])) + (parts[4] + parts[5])
            inverse = 1.0 / (1.0 + total)
            spot = at * rows + v
            for n, gained in enumerate(parts):
                weight[n, spot] = gained * inverse
            value = (tally_ref[tally, spot] * one - tally_ref[tally + 1, spot]) * inverse
            supply[spot] = value
            if turned:
                field[slot(at, v)] = value

    @pl.loop(0, span // half)
    def _(chunk):
        for n, copy in enumerate(time_copies):
            pl.when(chunk == n)(copy.wait_recv)
        for i in range(half):
            at = chunk * half + i
            weigh(at, i, twin_time, chain, other_weight, other_supply, other_field, 2, 1)
            weigh(at, i, chain, twin_time, chain_weight, chain_supply, chain_field, 0, 0)

    for v in range(rows):
        other_field[slot(-1, v)] = swing(other_field[slot(0, v)])

    def backward(count, dst, weight, supply, src, turned):
        cur = layer_of(src, 0)
        prev = [swing(one) for one in cur]
        for i in range(count):
            after_of = layer_of(src, i + 1)
            for v in range(rows):
                q = (i + 1 + v) % 2
                spot = i * rows + v
                acc = supply[spot] + weight[0, spot] * prev[v]
                acc = acc + weight[1, spot] * after_of[v]
                side = weight[2, spot] * y_down(cur, v) + weight[3, spot] * y_up(cur, v)
                across = across_z(cur[v], q ^ turned)
                acc = (acc + side) + (weight[4, spot] * cur[v] + weight[5, spot] * across)
                dst[slot(i, v)] = acc
            prev, cur = cur, after_of

    def rounds(first, times):
        count = half + ITERS - first

        @pl.loop(0, times)
        def _(_step):
            backward(count, chain_field, chain_weight, chain_supply, other_field, 0)
            backward(count - 1, other_field, other_weight, other_supply, chain_field, 1)

    rounds(2, 3)
    rounds(8, 2)
    rounds(12, 2)
    backward(half, chain_field, chain_weight, chain_supply, other_field, 0)

    for k in range(LOW):
        for t in range(0, depth, 2):
            low_side = k < LOW // 2
            near, next_to = (
                (half - 1 - (k * depth + t + n)) if low_side else (k * depth + t + n - half) for n in range(2)
            )
            for v in range(rows):
                a = chain_field[slot(near, v)]
                b = chain_field[slot(next_to, v)]
                both = jnp.where(upper, swing(b), a) if low_side else jnp.where(upper, b, swing(a))
                packed[k, t // 2, pl.ds(v, 8, stride=rows), :] = both

    keep = slots_ref.shape[2]

    def ship(k):
        c, b, p = peer(k)
        return remote(
            packed.at[p, :, pl.ds(c * keep, keep)], slots_ref.at[mine], send_sem.at[k], recv_sem.at[mine], c, b
        )

    for k in range(1, peers):
        ship(k).start()
    stay = pltpu.make_async_copy(
        packed.at[place, :, pl.ds(core * keep, keep)], slots_ref.at[mine], self_sem
    )
    stay.start()

    target = core - h + place // 2
    local = lax.rem(place, 2)

    def word(k):
        return remote(
            part.at[k], got_ref.at[local, h], part_send.at[k], part_recv.at[local, h], target, base + k
        )

    def home(k):
        return (target == core) & (place == k)

    for k in range(LOW):
        pl.when(jnp.logical_not(home(k)))(word(k).start)

        @pl.when(home(k))
        def _():
            got_ref[local, h] = part[k]

    def word_in(n, side):
        return remote(
            part.at[0], got_ref.at[n, side], part_send.at[0], part_recv.at[n, side], core, brick
        )

    for n in range(2):
        for side in range(2):
            from_me = (place == 2 * h + n) & (h == side)
            pl.when(jnp.logical_not(from_me))(word_in(n, side).wait_recv)
    for k in range(1, peers):
        m = lax.rem(mine + k, peers)
        remote(
            packed.at[0, :, pl.ds(0, keep)], slots_ref.at[m], send_sem.at[k], recv_sem.at[m], core, brick
        ).wait_recv()
    for k in range(1, peers):
        ship(k).wait_send()
    for k in range(LOW):
        pl.when(jnp.logical_not(home(k)))(word(k).wait_send)
    stay.wait()
    for copy in time_copies:
        copy.wait_send()


def finish_kernel(cores, slots_ref, got_ref, full_ref, out_ref, arr_ref):
    depth, keep, cells_z = out_ref.shape
    half_z = cells_z // 2
    first = lax.axis_index("brick") * depth
    row = pl.multiple_of(lax.axis_index("src") * keep, 8)
    lane = lax.broadcasted_iota(jnp.int32, (8, cells_z), 1)
    sub = lax.broadcasted_iota(jnp.int32, (8, cells_z), 0)
    upper = lane >= half_z
    plain = ((sub + jnp.where(upper, 1, 0)) & 1) == 0
    join = jnp.where((lane & 1) == 0, lane >> 1, cells_z - 1 - (lane >> 1))
    mirror = cells_z - 1 - lane
    for t in range(depth // 2):
        for y in range(0, keep, 8):
            sums = []
            for colour in range(2):
                total = None
                for c in range(colour, cores, 2):
                    for k in range(LOW):
                        one = slots_ref[c * LOW + k, t, pl.ds(y, 8), :]
                        total = one if total is None else total + one
                sums.append(total)
            even = jnp.where(plain, sums[0], sums[1])
            odd = jnp.where(plain, sums[1], sums[0])
            moved = jnp.take_along_axis(jnp.where(upper, even, odd), mirror, axis=1)
            for n, packed in enumerate((jnp.where(upper, moved, even), jnp.where(upper, odd, moved))):
                value = jnp.take_along_axis(packed, join, axis=1)
                slow = full_ref[first + 2 * t + n, pl.ds(row + y, 8), :]
                out_ref[2 * t + n, pl.ds(y, 8), :] = (slow * spacing) * value
    for n in range(2):
        arr_ref[pl.ds(n, 1), :] = got_ref[n, 0] + got_ref[n, 1]


def per_device(slowness, source_x, source_y, source_z, station_x, station_y, station_z, observed):
    bricks = lax.axis_size("brick")
    cores = lax.axis_size("src")
    depth, cells_y, cells_z = slowness.shape
    grid_x = depth * bricks
    rec = station_x.shape[0]
    rows = cells_y // 8
    ring = grid_x // 2
    half = LOW * depth // 2
    span = half + ITERS
    assert source_x.shape[0] == 2 and bricks % LOW == 0 and cores % 2 == 0
    assert half % 2 == 0 and span % half == 0 and span + 1 <= ring and (span * rows * 8) % TALLY == 0
    f32 = jnp.float32
    i32 = jnp.int32

    full, tally, code, spot = pl.pallas_call(
        functools.partial(gather_kernel, bricks),
        name="gather",
        out_shape=(
            jax.ShapeDtypeStruct((grid_x, cells_y, cells_z), f32),
            jax.ShapeDtypeStruct((4, span * rows, 8, cells_z), f32),
            jax.ShapeDtypeStruct((2, 1, rec), i32),
            jax.ShapeDtypeStruct((8, cells_z), i32),
        ),
        in_specs=[HBM] * 8,
        out_specs=(VMEM, VMEM, VMEM, VMEM),
        scratch_shapes=[
            pltpu.VMEM((4 * cells_z, rec), jnp.bfloat16),
            pltpu.SemaphoreType.DMA((2, bricks // LOW)),
            pltpu.SemaphoreType.DMA((3, bricks)),
            pltpu.SemaphoreType.DMA((bricks,)),
            pltpu.SemaphoreType.DMA((bricks,)),
            pltpu.SemaphoreType.DMA,
            pltpu.VMEM((1, rec), i32),
            pltpu.VMEM((1, rec), i32),
            pltpu.VMEM((1, rec), i32),
            pltpu.VMEM(observed.shape, f32),
            pltpu.SMEM((2,), i32),
            pltpu.SMEM((2,), i32),
            pltpu.SMEM((2,), i32),
            pltpu.SemaphoreType.DMA((7,)),
            pltpu.SemaphoreType.DMA((3,)),
            pltpu.SemaphoreType.DMA((3,)),
        ],
        compiler_params=pltpu.CompilerParams(
            collective_id=0, has_side_effects=True, vmem_limit_bytes=GATHER_VMEM
        ),
    )(
        *(
            pltpu.with_memory_space_constraint(a, pltpu.HBM)
            for a in (
                slowness,
                source_x,
                source_y,
                source_z,
                station_x[None],
                station_y[None],
                station_z[None],
                observed,
            )
        )
    )

    share = rec // bricks
    quarter = share * LOW
    keep = cells_y // cores
    layer = (rows, 8, cells_z)
    ring_shape = ((ring + 2) * rows, 8, cells_z)
    slots, got = pl.pallas_call(
        functools.partial(solve_kernel, depth, cores),
        name="solve",
        out_shape=(
            jax.ShapeDtypeStruct((LOW * cores, depth // 2, keep, cells_z), f32),
            jax.ShapeDtypeStruct((2, 2, 1, share), f32),
        ),
        in_specs=[VMEM] * 4,
        out_specs=(VMEM, VMEM),
        scratch_shapes=[
            pltpu.VMEM(ring_shape, f32),
            pltpu.VMEM(ring_shape, f32),
            pltpu.VMEM((ring * rows, 8, cells_z), f32),
            pltpu.VMEM((ring * rows, 8, cells_z), f32),
            pltpu.VMEM(((span + 2) * rows, 8, cells_z), f32),
            pltpu.VMEM((6, span * rows, 8, cells_z), f32),
            pltpu.VMEM((6, span * rows, 8, cells_z), f32),
            pltpu.VMEM((span * rows, 8, cells_z), f32),
            pltpu.VMEM((span * rows, 8, cells_z), f32),
            pltpu.VMEM(((span + 2) * rows, 8, cells_z), f32),
            pltpu.VMEM(((span + 2) * rows, 8, cells_z), f32),
            pltpu.VMEM((LOW, depth // 2, cells_y, cells_z), f32),
            pltpu.VMEM((quarter, cells_z), f32),
            pltpu.VMEM((LOW, 1, share), f32),
            pltpu.SMEM((1, rec), i32),
            pltpu.SemaphoreType.DMA,
            pltpu.SemaphoreType.DMA((span // half,)),
            pltpu.SemaphoreType.DMA((span // half,)),
            pltpu.SemaphoreType.DMA((LOW * cores,)),
            pltpu.SemaphoreType.DMA((LOW * cores,)),
            pltpu.SemaphoreType.DMA((LOW,)),
            pltpu.SemaphoreType.DMA((2, 2)),
            pltpu.SemaphoreType.DMA,
        ],
        compiler_params=pltpu.CompilerParams(
            collective_id=1, has_side_effects=True, vmem_limit_bytes=SOLVE_VMEM
        ),
    )(code, spot, full, tally)

    return tuple(
        pl.pallas_call(
            functools.partial(finish_kernel, cores),
            name="finish",
            out_shape=(
                jax.ShapeDtypeStruct((depth, keep, cells_z), f32),
                jax.ShapeDtypeStruct((2, share), f32),
            ),
            in_specs=[VMEM] * 3,
            compiler_params=pltpu.CompilerParams(vmem_limit_bytes=FINISH_VMEM),
        )(slots, got, full)
    )


def solution(mesh):
    in_specs = (P("brick", None, None), P("src"), P("src"), P("src"), P(), P(), P(), P("src", None))
    out_specs = (P("brick", "src", None), P("src", "brick"))
    return jax.shard_map(
        per_device, mesh=mesh, in_specs=in_specs, out_specs=out_specs, check_vma=False
    )
```

```python
import functools

import jax
import jax.numpy as jnp
from jax import lax
from jax.experimental import pallas as pl
from jax.experimental.pallas import tpu as pltpu
from jax.sharding import PartitionSpec as P

ITERS = 16

spacing = 0.015625
big_value = 1000000.0
start_slowness = 2.0
half_step = 0.5 * spacing
LOW = 4
SOLVE_VMEM = 40 << 20
FINISH_VMEM = 8 << 20
TALLY = 512
REACH = 2

VMEM = pl.BlockSpec(memory_space=pltpu.VMEM)
SMEM = pl.BlockSpec(memory_space=pltpu.SMEM)
HBM = pl.BlockSpec(memory_space=pltpu.HBM)
MESH = pl.DeviceIdType.MESH


def remote(src, dst, send_sem, recv_sem, core, brick):
    return pltpu.make_async_remote_copy(
        src_ref=src,
        dst_ref=dst,
        send_sem=send_sem,
        recv_sem=recv_sem,
        device_id={"src": core, "brick": brick},
        device_id_type=MESH,
    )


def solve_kernel(
    bricks,
    cores,
    slow_ref,
    sx_ref,
    sy_ref,
    sz_ref,
    stx_ref,
    sty_ref,
    stz_ref,
    obs_ref,
    slots_ref,
    got_ref,
    own_ref,
    full_ref,
    tally_ref,
    code_ref,
    spot_ref,
    table,
    chain,
    other,
    chain_cost,
    other_cost,
    twin_time,
    chain_weight,
    other_weight,
    chain_supply,
    other_supply,
    chain_field,
    other_field,
    packed,
    picked,
    part,
    stx_buf,
    sty_buf,
    stz_buf,
    seen_buf,
    code,
    sx_buf,
    sy_buf,
    sz_buf,
    line_sem,
    brick_send,
    brick_recv,
    twin_sem,
    own_sem,
    in_sem,
    word_send,
    word_recv,
    code_sem,
    time_send,
    time_recv,
    send_sem,
    recv_sem,
    part_send,
    part_recv,
    self_sem,
):
    grid_x, cells_y, cells_z = full_ref.shape
    depth = slow_ref.shape[0]
    half_depth = depth // 2
    lines = bricks // LOW
    reach = REACH if lines == REACH + 2 else lines - 1
    early = reach < lines - 1
    rows = cells_y // 8
    shift = rows.bit_length() - 1
    ring = grid_x // 2
    block = LOW * depth
    half = block // 2
    span = half + ITERS
    half_z = cells_z // 2
    me = lax.axis_index("brick")
    core = lax.axis_index("src")
    h = lax.rem(core, 2)
    twin = core + 1 - 2 * h
    line = me // LOW
    place = lax.rem(me, LOW)
    base = line * LOW
    peers = LOW * cores
    mine = core * LOW + place
    centre = line * block + half
    bit_x = lax.rem(me, 2)
    bit_y = lax.rem(me // 2, 2)
    flip_x = 1 - 2 * bit_x
    flip_y = 2 - 4 * bit_y
    first = me + flip_x * (1 - h) + flip_y * h
    second = me + flip_y * (1 - h) + flip_x * h
    corner = me + flip_x + flip_y
    owner = place // 2 == h
    local = lax.rem(place, 2)

    barrier = pltpu.get_barrier_semaphore()

    def greet(c, b):
        pl.semaphore_signal(barrier, inc=1, device_id={"src": c, "brick": b}, device_id_type=MESH)

    def peer(k):
        t = lax.rem(mine + k, peers)
        return t // LOW, base + lax.rem(t, LOW), lax.rem(t, LOW)

    for k in range(1, peers):
        c, b, _ = peer(k)
        greet(c, b)
    for k in range(1, reach + 1):
        pl.when(line >= k)(lambda k=k: greet(core, me - LOW * k))
        pl.when(line + k < lines)(lambda k=k: greet(core, me + LOW * k))

    stations = [
        pltpu.make_async_copy(src, dst, in_sem.at[k])
        for k, (src, dst) in enumerate(((stx_ref, stx_buf), (sty_ref, sty_buf), (stz_ref, stz_buf)))
    ]
    spots = [
        pltpu.make_async_copy(src, dst, in_sem.at[3 + k])
        for k, (src, dst) in enumerate(((sx_ref, sx_buf), (sy_ref, sy_buf), (sz_ref, sz_buf)))
    ]
    seen_copy = pltpu.make_async_copy(obs_ref, seen_buf, in_sem.at[6])
    for load in stations:
        load.start()

    @pl.when(owner)
    def _():
        for load in spots:
            load.start()
        seen_copy.start()

    def piece(q, part):
        return full_ref.at[pl.ds(q * depth + part * half_depth, half_depth)]

    def copy(kind, q, brick, own=False):
        src = slow_ref.at[pl.ds(h * half_depth, half_depth)] if own else piece(q, h)
        return remote(src, piece(q, h), brick_send.at[kind, q], brick_recv.at[q], core, brick)

    def twin_copy(q):
        return remote(piece(q, h), piece(q, h), brick_send.at[2, q], twin_sem.at[q], twin, me)

    def along(k, up):
        dst = piece(me, h)
        src = slow_ref.at[pl.ds(h * half_depth, half_depth)]
        brick = me + LOW * k if up else me - LOW * k
        return remote(src, dst, line_sem.at[int(up), k], brick_recv.at[me], core, brick)

    def own_line(k, wait):
        def go(up):
            c = along(k, up)
            c.wait_send() if wait else c.start()

        pl.when(line >= k)(lambda: go(False))
        pl.when(line + k < lines)(lambda: go(True))

    def sends(q, own, wait):
        for kind, brick in ((0, first), (1, second)):
            c = copy(kind, q, brick, own)
            c.wait_send() if wait else c.start()

    own_copy = pltpu.make_async_copy(slow_ref, full_ref.at[pl.ds(me * depth, depth)], own_sem)
    seen_send = remote(obs_ref, seen_buf, word_send.at[0], word_recv.at[0], twin, me)
    spot_send = remote(spot_ref, spot_ref, word_send.at[1], word_recv.at[1], twin, me)

    near = jnp.minimum(line, reach) + jnp.minimum(lines - 1 - line, reach)
    pl.semaphore_wait(barrier, near + peers - 1)
    pl.when(owner)(seen_send.start)
    for k in range(1, reach + 1):
        own_line(k, False)
        if k == 1:
            sends(me, True, False)
    own_copy.start()

    def arrived(q):
        remote(piece(q, h), piece(q, h), brick_send.at[0, q], brick_recv.at[q], core, first).wait_recv()

    def on_line(base, i, act):
        pl.when((i <= reach) & (line >= i))(lambda: act(base - LOW * i, -1))
        pl.when((i <= reach) & (line + i < lines))(lambda: act(base + LOW * i, 1))

    def both(base, i, act):
        pl.when(i == 0)(lambda: act(base, 0))
        pl.when(i > 0)(lambda: on_line(base, i, act))

    def is_far(i):
        return (i == reach) & early

    def from_line(wait, i):
        def act(q, side):
            if not wait:
                arrived(q)
            sends(q, False, wait)

            @pl.when(is_far(i))
            def _():
                c = copy(3, q, corner)
                c.wait_send() if wait else c.start()

            c = twin_copy(q)
            c.wait_send() if wait else c.start()

        return act

    def from_first(wait, i):
        def act(q, side):
            if not wait:
                arrived(q)

            @pl.when(jnp.logical_not(is_far(i)))
            def _():
                c = copy(1, q, second)
                c.wait_send() if wait else c.start()

            c = twin_copy(q)
            c.wait_send() if wait else c.start()

        return act

    def from_second(wait):
        def act(q, side):
            if not wait:
                arrived(q)
            c = twin_copy(q)
            c.wait_send() if wait else c.start()

        return act

    def turn(i, wait):
        on_line(me, i, from_line(wait, i))
        both(first, i - 1, from_first(wait, i - 1))
        both(second, i - 1, from_second(wait))
        pl.when(i >= 2)(lambda: both(corner, i - 2, from_second(wait)))

    @pl.when(owner)
    def _():
        for load in spots:
            load.wait()
        sub = lax.broadcasted_iota(jnp.int32, spot_ref.shape, 0)
        spot_ref[...] = jnp.where(
            sub == 0, sx_buf[local], jnp.where(sub == 1, sy_buf[local], sz_buf[local])
        )

    for load in stations:
        load.wait()
    sty = sty_buf[...]
    stz = stz_buf[...]
    stx = stx_buf[...]
    away = stx - centre
    away = jnp.where(away < 0, away + grid_x, away)
    beyond = away < ring
    step_x = jnp.where(beyond, away, grid_x - 1 - away)
    row = (step_x * rows + (sty & (rows - 1))) * 8 + (sty >> shift)
    column = jnp.where(beyond, cells_z - 1 - (stz >> 1), stz >> 1)
    column = jnp.where(((stx + sty + stz) & 1) == h, column, -1)
    code_ref[0] = row
    code_ref[1] = column
    load_code = pltpu.make_async_copy(code_ref.at[0], code, code_sem)
    load_code.start()
    rec = row.shape[1]
    hit = lax.broadcasted_iota(jnp.int32, (cells_z, rec), 0) == column

    pl.when(owner)(seen_copy.wait)
    pl.when(owner)(spot_send.start)
    pl.when(jnp.logical_not(owner))(seen_send.wait_recv)
    seen = seen_buf[pl.ds(local, 1), :] * (1.0 / spacing)
    hi = seen.astype(jnp.bfloat16).astype(jnp.float32)
    rest = seen - hi
    mid = rest.astype(jnp.bfloat16).astype(jnp.float32)
    lo = rest - mid
    for n, value in enumerate((jnp.ones_like(seen), hi, mid, lo)):
        table[pl.ds(n * cells_z, cells_z), :] = jnp.where(hit, value, 0.0).astype(jnp.bfloat16)

    tiles = TALLY // 8
    blocks = tally_ref.shape[1] // tiles

    def tally(step):
        rows_of = lax.broadcasted_iota(jnp.int32, (TALLY, rec), 0) + step * TALLY
        pick = jnp.where(rows_of == row, 1.0, 0.0).astype(jnp.bfloat16)
        got = lax.dot_general(
            pick, table[...], (((1,), (1,)), ((), ())), preferred_element_type=jnp.float32
        )
        spot = pl.ds(step * tiles, tiles)
        tally_ref[0, spot] = got[:, :cells_z].reshape(tiles, 8, cells_z)
        total = got[:, cells_z : 2 * cells_z] + (
            got[:, 2 * cells_z : 3 * cells_z] + got[:, 3 * cells_z :]
        )
        tally_ref[1, spot] = total.reshape(tiles, 8, cells_z)

    tally_send = remote(
        tally_ref.at[pl.ds(0, 2)], tally_ref.at[pl.ds(2, 2)], word_send.at[2], word_recv.at[2], twin, me
    )

    def twins(low, high):
        @pl.loop(0, bricks)
        def _(q):
            gap = jnp.maximum(q // LOW - line, line - q // LOW)

            @pl.when((q != me) & (gap >= low) & (gap <= high))
            def _():
                remote(
                    piece(q, 1 - h), piece(q, 1 - h), brick_send.at[2, q], twin_sem.at[q], twin, me
                ).wait_recv()

    turns = reach if early else reach + 2

    @pl.loop(0, max(turns, blocks))
    def _(step):
        pl.when(step < turns)(lambda: turn(step + 1, False))
        pl.when(step < blocks)(lambda: tally(step))

    if early:
        for gap in range(reach + 1, lines):
            for away_line in (line - gap, line + gap):

                @pl.when((away_line >= 0) & (away_line < lines))
                def _():
                    @pl.loop(0, block)
                    def _(x):
                        full_ref[away_line * block + x] = jnp.ones((cells_y, cells_z), jnp.float32)

        both(corner, reach - 1, from_second(False))
    tally_send.start()
    own_copy.wait()
    twins(0, reach - 1 if early else reach)

    share = got_ref.shape[-1]
    quarter = picked.shape[0]
    pl.when(jnp.logical_not(owner))(spot_send.wait_recv)
    keep = slots_ref.shape[2]
    for t in range(depth):
        own_ref[t] = full_ref[me * depth + t, pl.ds(pl.multiple_of(core * keep, 8), keep), :]

    picks = ((line > 0) & (line < lines - 1)) if early else line >= 0

    def pick_line(n):
        if not early:
            return line
        return (line - 1) * 2 + n

    lane = lax.broadcasted_iota(jnp.int32, (8, cells_z), 1)
    sub = lax.broadcasted_iota(jnp.int32, (8, cells_z), 0)
    sub_first = sub == 0
    sub_last = sub == 7
    upper = lane >= half_z
    inner = jnp.where(upper, cells_z - 1 - lane, lane)
    parity = [lax.rem(q + h, 2) for q in range(2)]
    cell_z = [inner * 2 + jnp.where(upper, 1 - p, p) for p in parity]
    from_low = [(lane & 1) == p for p in parity]
    edge_z = [(lane & (half_z - 1)) == p * (half_z - 1) for p in parity]
    slide = [1 + p * (cells_z - 2) for p in parity]
    mirror = cells_z - 1 - lane

    def slot(i, v):
        return (i + 1) * rows + v

    sx = spot_ref[0:1, :]
    sy = spot_ref[1:2, :]
    sz = spot_ref[2:3, :]
    unit = (start_slowness * spacing) ** 2
    flat = []
    for q in range(2):
        dz = (cell_z[q] - sz).astype(jnp.float32)
        dz = dz * dz
        for v in range(rows):
            dy = (sub * rows + v - sy).astype(jnp.float32)
            flat.append((dy * dy + dz) * unit)

    def prepare(quad):
        for j in range(4):
            i = quad * 4 + j
            x_low = centre - 1 - i
            x_low = jnp.where(x_low < 0, x_low + grid_x, x_low)
            x_high = centre + i
            x_high = jnp.where(x_high >= grid_x, x_high - grid_x, x_high)
            dx = (jnp.where(upper, x_high, x_low) - sx).astype(jnp.float32)
            dx = dx * dx * unit
            for v in range(rows):
                q = (j + 1 + v) % 2
                low = full_ref[x_low, pl.ds(v, 8, stride=rows), :]
                high = full_ref[x_high, pl.ds(v, 8, stride=rows), :]
                pair_of = (
                    (chain, chain_cost, q, jnp.where(from_low[q], low, high)),
                    (other, other_cost, 1 - q, jnp.where(from_low[q], high, low)),
                )
                for field, cost, k, natural in pair_of if q else pair_of[::-1]:
                    slow = jnp.take_along_axis(natural, cell_z[k], axis=1)
                    square = dx + flat[k * rows + v]
                    start = square * lax.rsqrt(jnp.maximum(square, unit * 0.5))
                    cost[i * rows + v] = (2.0 * half_step) * slow
                    field[slot(i, v)] = start + half_step * slow

    @pl.loop(0, (span if early else ring) // 4)
    def _(quad):
        prepare(quad)

    cuts = {
        b: jnp.where(upper, grid_x - centre, centre) == b for b in range(half, ring, half) if (b // half) % 2
    }

    def swing(one):
        return jnp.take_along_axis(one, mirror, axis=1)

    def across_z(one, k):
        return pltpu.roll(one, slide[k], 1)

    def y_up(cur, v):
        return cur[v + 1] if v + 1 < rows else pltpu.roll(cur[0], 7, 0)

    def y_down(cur, v):
        return cur[v - 1] if v else pltpu.roll(cur[rows - 1], 1, 0)

    def layer_of(ref, i):
        return [ref[slot(i, v)] for v in range(rows)]

    def sweep(dst, cost, src, turned, low_end, high_end):
        cur = layer_of(src, low_end)
        prev = layer_of(src, low_end - 1) if low_end else [swing(one) for one in cur]
        for i in range(low_end, high_end):
            after_of = layer_of(src, i + 1) if i + 1 < ring else [swing(one) for one in cur]
            for v in range(rows):
                q = (i + 1 + v) % 2
                before = prev[v]
                after = after_of[v]
                if i in cuts:
                    before = jnp.where(cuts[i], big_value, before)
                if i + 1 in cuts:
                    after = jnp.where(cuts[i + 1], big_value, after)
                up = y_up(cur, v)
                down = y_down(cur, v)
                if v + 1 == rows:
                    up = jnp.where(sub_last, big_value, up)
                if v == 0:
                    down = jnp.where(sub_first, big_value, down)
                k = q ^ turned
                across = jnp.where(edge_z[k], cur[v], across_z(cur[v], k))
                low = jnp.minimum(across, cur[v])
                for value in (before, after, down, up):
                    low = jnp.minimum(low, value)
                dst[slot(i, v)] = jnp.minimum(dst[slot(i, v)], low + cost[i * rows + v])
            prev, cur = cur, after_of

    assert ITERS % 2 == 0

    def step_of(j, low_end, high_end):
        if j % 2:
            sweep(other, other_cost, chain, 1, low_end, high_end)
        else:
            sweep(chain, chain_cost, other, 0, low_end, high_end)

    if early:
        for j in range(1, ITERS + 1):
            step_of(j, 0, span - j)
            if j == ITERS // 2:
                both(first, reach, from_first(False, reach))
                both(second, reach, from_second(False))
        both(corner, reach, from_second(False))
        twins(reach, reach)

        @pl.loop(span // 4, ring // 4)
        def _(quad):
            prepare(quad)

        for j in range(1, ITERS + 1):
            step_of(j, span - j, ring)
    else:

        @pl.loop(0, ITERS // 2)
        def _(_step):
            step_of(1, 0, ring)
            step_of(2, 0, ring)

    @pl.loop(0, ring)
    def _(i):
        for v in range(rows):
            chain[slot(i, v)] = (chain[slot(i, v)] - 0.5 * chain_cost[i * rows + v]) * (1.0 / spacing)

    for v in range(rows):
        chain[slot(-1, v)] = swing(chain[slot(0, v)])

    stops = [0] + [(2 + n * half) * rows for n in range(1, span // half + 1)]
    time_copies = []
    for n, (low, high) in enumerate(zip(stops, stops[1:])):
        part_of = pl.ds(low, high - low)
        time_copies.append(
            remote(chain.at[part_of], twin_time.at[part_of], time_send.at[n], time_recv.at[n], twin, me)
        )
    for copy_of in time_copies:
        copy_of.start()

    load_code.wait()
    unroll = 16

    def pick(n):
        whose = pick_line(n)
        place_of = pl.multiple_of(whose * quarter, 128)

        @pl.loop(0, quarter // unroll)
        def _(m):
            for j in range(unroll):
                r = m * unroll + j
                at = code[0, place_of + r]
                picked[pl.ds(r, 1), :] = chain[(at >> 3) + rows, pl.ds(at & 7, 1), :]

        column = code_ref[1, :, pl.ds(place_of, quarter)]
        turned = jnp.transpose(picked[...])
        here = lax.broadcasted_iota(jnp.int32, turned.shape, 0) == column
        arrived_at = jnp.sum(jnp.where(here, turned, 0.0), axis=0, keepdims=True) * spacing
        for k in range(LOW):
            part[n * LOW + k] = arrived_at[:, k * share : (k + 1) * share]

    pl.when(picks)(lambda: pick(0))

    for v in range(rows):
        chain_field[slot(span - 2, v)] = jnp.zeros((8, cells_z), jnp.float32)
        chain_field[slot(span - 1, v)] = jnp.zeros((8, cells_z), jnp.float32)
        chain_field[slot(span, v)] = jnp.zeros((8, cells_z), jnp.float32)
        other_field[slot(span, v)] = jnp.zeros((8, cells_z), jnp.float32)

    bound = jnp.where(upper, grid_x - centre, centre)
    tally_send.wait_recv()

    def weigh(at, i, own, theirs, weight, supply, field, tally, turned):
        cur = [theirs[slot(at, v)] for v in range(rows)]
        cut_before = bound == at
        cut_after = bound == at + 1
        for v in range(rows):
            q = (i + 1 + v) % 2
            one = own[slot(at, v)]

            def gain(value):
                return jnp.maximum(value - one, 0.0)

            before = gain(theirs[slot(at - 1, v)])
            after = gain(theirs[slot(at + 1, v)])
            if i % half == 0:
                before = jnp.where(cut_before, 0.0, before)
            if (i + 1) % half == 0:
                after = jnp.where(cut_after, 0.0, after)
            up = gain(y_up(cur, v))
            down = gain(y_down(cur, v))
            if v + 1 == rows:
                up = jnp.where(sub_last, 0.0, up)
            if v == 0:
                down = jnp.where(sub_first, 0.0, down)
            k = q ^ turned
            across = jnp.where(edge_z[k], 0.0, gain(across_z(cur[v], k)))
            parts = (before, after, down, up, gain(cur[v]), across)
            total = ((parts[0] + parts[1]) + (parts[2] + parts[3])) + (parts[4] + parts[5])
            inverse = 1.0 / (1.0 + total)
            spot = at * rows + v
            for n, gained in enumerate(parts):
                weight[n, spot] = gained * inverse
            value = (tally_ref[tally, spot] * one - tally_ref[tally + 1, spot]) * inverse
            supply[spot] = value
            if turned:
                field[slot(at, v)] = value

    @pl.loop(0, span // half)
    def _(chunk):
        for n, copy_of in enumerate(time_copies):
            pl.when(chunk == n)(copy_of.wait_recv)
        for i in range(half):
            at = chunk * half + i
            weigh(at, i, twin_time, chain, other_weight, other_supply, other_field, 2, 1)
            weigh(at, i, chain, twin_time, chain_weight, chain_supply, chain_field, 0, 0)

    for v in range(rows):
        other_field[slot(-1, v)] = swing(other_field[slot(0, v)])

    def backward(count, dst, weight, supply, src, turned):
        cur = layer_of(src, 0)
        prev = [swing(one) for one in cur]
        for i in range(count):
            after_of = layer_of(src, i + 1)
            for v in range(rows):
                q = (i + 1 + v) % 2
                spot = i * rows + v
                acc = supply[spot] + weight[0, spot] * prev[v]
                acc = acc + weight[1, spot] * after_of[v]
                side = weight[2, spot] * y_down(cur, v) + weight[3, spot] * y_up(cur, v)
                across = across_z(cur[v], q ^ turned)
                acc = (acc + side) + (weight[4, spot] * cur[v] + weight[5, spot] * across)
                dst[slot(i, v)] = acc
            prev, cur = cur, after_of

    def rounds(first, times):
        count = half + ITERS - first

        @pl.loop(0, times)
        def _(_step):
            backward(count, chain_field, chain_weight, chain_supply, other_field, 0)
            backward(count - 1, other_field, other_weight, other_supply, chain_field, 1)

    rounds(2, 3)
    rounds(8, 2)
    rounds(12, 2)
    backward(half, chain_field, chain_weight, chain_supply, other_field, 0)

    for k in range(LOW):
        for t in range(0, depth, 2):
            low_side = k < LOW // 2
            near, next_to = (
                (half - 1 - (k * depth + t + n)) if low_side else (k * depth + t + n - half) for n in range(2)
            )
            for v in range(rows):
                a = chain_field[slot(near, v)]
                b = chain_field[slot(next_to, v)]
                merged = jnp.where(upper, swing(b), a) if low_side else jnp.where(upper, b, swing(a))
                packed[k, t // 2, pl.ds(v, 8, stride=rows), :] = merged

    keep = slots_ref.shape[2]

    def ship(k):
        c, b, p = peer(k)
        return remote(
            packed.at[p, :, pl.ds(c * keep, keep)], slots_ref.at[mine], send_sem.at[k], recv_sem.at[mine], c, b
        )

    for k in range(1, peers):
        ship(k).start()
    stay = pltpu.make_async_copy(
        packed.at[place, :, pl.ds(core * keep, keep)], slots_ref.at[mine], self_sem
    )
    stay.start()

    target = core - h + place // 2

    def word(n, k):
        return remote(
            part.at[n * LOW + k],
            got_ref.at[local, h],
            part_send.at[n * LOW + k],
            part_recv.at[local, h],
            target,
            pick_line(n) * LOW + k,
        )

    def home(n, k):
        return (target == core) & (pick_line(n) * LOW + k == me)

    def post(n):
        for k in range(LOW):
            pl.when(jnp.logical_not(home(n, k)))(word(n, k).start)

            @pl.when(home(n, k))
            def _():
                got_ref[local, h] = part[n * LOW + k]

    def posted(n):
        for k in range(LOW):
            pl.when(jnp.logical_not(home(n, k)))(word(n, k).wait_send)

    pl.when(picks)(lambda: post(0))
    if early:
        pl.when(picks)(lambda: pick(1))
        pl.when(picks)(lambda: post(1))

    def word_in(n, side):
        return remote(
            part.at[0], got_ref.at[n, side], part_send.at[0], part_recv.at[n, side], core, me
        )

    for n in range(2):
        for side in range(2):
            from_me = picks & (place == 2 * h + n) & (h == side)
            pl.when(jnp.logical_not(from_me))(word_in(n, side).wait_recv)
    for k in range(1, peers):
        m = lax.rem(mine + k, peers)
        remote(
            packed.at[0, :, pl.ds(0, keep)], slots_ref.at[m], send_sem.at[k], recv_sem.at[m], core, me
        ).wait_recv()
    for k in range(1, peers):
        ship(k).wait_send()
    pl.when(picks)(lambda: posted(0))
    if early:
        pl.when(picks)(lambda: posted(1))
    stay.wait()
    for copy_of in time_copies:
        copy_of.wait_send()
    tally_send.wait_send()
    sends(me, True, True)
    for k in range(1, reach + 1):
        own_line(k, True)

    @pl.loop(1, reach + 3)
    def _(i):
        turn(i, True)

    @pl.when(owner)
    def _():
        seen_send.wait_send()
        spot_send.wait_send()


def finish_kernel(cores, slots_ref, got_ref, own_ref, out_ref, arr_ref):
    depth, keep, cells_z = out_ref.shape
    half_z = cells_z // 2
    lane = lax.broadcasted_iota(jnp.int32, (8, cells_z), 1)
    sub = lax.broadcasted_iota(jnp.int32, (8, cells_z), 0)
    upper = lane >= half_z
    plain = ((sub + jnp.where(upper, 1, 0)) & 1) == 0
    join = jnp.where((lane & 1) == 0, lane >> 1, cells_z - 1 - (lane >> 1))
    mirror = cells_z - 1 - lane
    for t in range(depth // 2):
        for y in range(0, keep, 8):
            sums = []
            for colour in range(2):
                total = None
                for c in range(colour, cores, 2):
                    for k in range(LOW):
                        one = slots_ref[c * LOW + k, t, pl.ds(y, 8), :]
                        total = one if total is None else total + one
                sums.append(total)
            even = jnp.where(plain, sums[0], sums[1])
            odd = jnp.where(plain, sums[1], sums[0])
            moved = jnp.take_along_axis(jnp.where(upper, even, odd), mirror, axis=1)
            for n, packed in enumerate((jnp.where(upper, moved, even), jnp.where(upper, odd, moved))):
                value = jnp.take_along_axis(packed, join, axis=1)
                slow = own_ref[2 * t + n, pl.ds(y, 8), :]
                out_ref[2 * t + n, pl.ds(y, 8), :] = (slow * spacing) * value
    for n in range(2):
        arr_ref[pl.ds(n, 1), :] = got_ref[n, 0] + got_ref[n, 1]


def per_device(slowness, source_x, source_y, source_z, station_x, station_y, station_z, observed):
    bricks = lax.axis_size("brick")
    cores = lax.axis_size("src")
    depth, cells_y, cells_z = slowness.shape
    grid_x = depth * bricks
    rec = station_x.shape[0]
    rows = cells_y // 8
    ring = grid_x // 2
    half = LOW * depth // 2
    span = half + ITERS
    assert source_x.shape[0] == 2 and bricks % LOW == 0 and cores % 2 == 0
    assert half % 2 == 0 and span % half == 0 and span + 1 <= ring and (span * rows * 8) % TALLY == 0
    assert span % 4 == 0 and ring % 4 == 0
    f32 = jnp.float32
    i32 = jnp.int32
    share = rec // bricks
    quarter = share * LOW
    keep = cells_y // cores
    ring_shape = ((ring + 2) * rows, 8, cells_z)
    span_shape = ((span + 2) * rows, 8, cells_z)
    dma = pltpu.SemaphoreType.DMA
    slots, got, own = pl.pallas_call(
        functools.partial(solve_kernel, bricks, cores),
        name="solve",
        out_shape=(
            jax.ShapeDtypeStruct((LOW * cores, depth // 2, keep, cells_z), f32),
            jax.ShapeDtypeStruct((2, 2, 1, share), f32),
            jax.ShapeDtypeStruct((depth, keep, cells_z), f32),
        ),
        in_specs=[HBM] * 8,
        out_specs=(VMEM, VMEM, VMEM),
        scratch_shapes=[
            pltpu.VMEM((grid_x, cells_y, cells_z), f32),
            pltpu.VMEM((4, span * rows, 8, cells_z), f32),
            pltpu.VMEM((2, 1, rec), i32),
            pltpu.VMEM((8, cells_z), i32),
            pltpu.VMEM((4 * cells_z, rec), jnp.bfloat16),
            pltpu.VMEM(ring_shape, f32),
            pltpu.VMEM(ring_shape, f32),
            pltpu.VMEM((ring * rows, 8, cells_z), f32),
            pltpu.VMEM((ring * rows, 8, cells_z), f32),
            pltpu.VMEM(span_shape, f32),
            pltpu.VMEM((6, span * rows, 8, cells_z), f32),
            pltpu.VMEM((6, span * rows, 8, cells_z), f32),
            pltpu.VMEM((span * rows, 8, cells_z), f32),
            pltpu.VMEM((span * rows, 8, cells_z), f32),
            pltpu.VMEM(span_shape, f32),
            pltpu.VMEM(span_shape, f32),
            pltpu.VMEM((LOW, depth // 2, cells_y, cells_z), f32),
            pltpu.VMEM((quarter, cells_z), f32),
            pltpu.VMEM((2 * LOW, 1, share), f32),
            pltpu.VMEM((1, rec), i32),
            pltpu.VMEM((1, rec), i32),
            pltpu.VMEM((1, rec), i32),
            pltpu.VMEM(observed.shape, f32),
            pltpu.SMEM((1, rec), i32),
            pltpu.SMEM((2,), i32),
            pltpu.SMEM((2,), i32),
            pltpu.SMEM((2,), i32),
            dma((2, bricks // LOW)),
            dma((4, bricks)),
            dma((bricks,)),
            dma((bricks,)),
            dma,
            dma((7,)),
            dma((3,)),
            dma((3,)),
            dma,
            dma((span // half,)),
            dma((span // half,)),
            dma((LOW * cores,)),
            dma((LOW * cores,)),
            dma((2 * LOW,)),
            dma((2, 2)),
            dma,
        ],
        compiler_params=pltpu.CompilerParams(
            collective_id=0, has_side_effects=True, vmem_limit_bytes=SOLVE_VMEM
        ),
    )(
        *(
            pltpu.with_memory_space_constraint(a, pltpu.HBM)
            for a in (
                slowness,
                source_x,
                source_y,
                source_z,
                station_x[None],
                station_y[None],
                station_z[None],
                observed,
            )
        )
    )

    return tuple(
        pl.pallas_call(
            functools.partial(finish_kernel, cores),
            name="finish",
            out_shape=(
                jax.ShapeDtypeStruct((depth, keep, cells_z), f32),
                jax.ShapeDtypeStruct((2, share), f32),
            ),
            in_specs=[VMEM] * 3,
            compiler_params=pltpu.CompilerParams(vmem_limit_bytes=FINISH_VMEM),
        )(slots, got, own)
    )


def solution(mesh):
    in_specs = (P("brick", None, None), P("src"), P("src"), P("src"), P(), P(), P(), P("src", None))
    out_specs = (P("brick", "src", None), P("src", "brick"))
    return jax.shard_map(
        per_device, mesh=mesh, in_specs=in_specs, out_specs=out_specs, check_vma=False
    )
```

```python
import functools

import jax
import jax.numpy as jnp
from jax import lax
from jax.experimental import pallas as pl
from jax.experimental.pallas import tpu as pltpu
from jax.sharding import PartitionSpec as P

ITERS = 16

spacing = 0.015625
big_value = 1000000.0
start_slowness = 2.0
half_step = 0.5 * spacing
LOW = 4
SOLVE_VMEM = 40 << 20
FINISH_VMEM = 8 << 20
TALLY = 512
REACH = 2

VMEM = pl.BlockSpec(memory_space=pltpu.VMEM)
SMEM = pl.BlockSpec(memory_space=pltpu.SMEM)
HBM = pl.BlockSpec(memory_space=pltpu.HBM)
MESH = pl.DeviceIdType.MESH


def remote(src, dst, send_sem, recv_sem, core, brick):
    return pltpu.make_async_remote_copy(
        src_ref=src,
        dst_ref=dst,
        send_sem=send_sem,
        recv_sem=recv_sem,
        device_id={"src": core, "brick": brick},
        device_id_type=MESH,
    )


def solve_kernel(
    bricks,
    cores,
    slow_ref,
    sx_ref,
    sy_ref,
    sz_ref,
    stx_ref,
    sty_ref,
    stz_ref,
    obs_ref,
    slots_ref,
    got_ref,
    own_ref,
    full_ref,
    tally_ref,
    code_ref,
    spot_ref,
    table,
    chain,
    other,
    chain_cost,
    other_cost,
    twin_time,
    chain_weight,
    other_weight,
    chain_supply,
    other_supply,
    chain_field,
    other_field,
    packed,
    picked,
    part,
    stx_buf,
    sty_buf,
    stz_buf,
    seen_buf,
    code,
    sx_buf,
    sy_buf,
    sz_buf,
    line_sem,
    brick_send,
    brick_recv,
    twin_sem,
    own_sem,
    in_sem,
    word_send,
    word_recv,
    code_sem,
    time_send,
    time_recv,
    send_sem,
    recv_sem,
    part_send,
    part_recv,
    self_sem,
):
    grid_x, cells_y, cells_z = full_ref.shape
    depth = slow_ref.shape[0]
    half_depth = depth // 2
    lines = bricks // LOW
    reach = REACH if lines == REACH + 2 else lines - 1
    early = reach < lines - 1
    rows = cells_y // 8
    shift = rows.bit_length() - 1
    ring = grid_x // 2
    block = LOW * depth
    half = block // 2
    span = half + ITERS
    half_z = cells_z // 2
    me = lax.axis_index("brick")
    core = lax.axis_index("src")
    h = lax.rem(core, 2)
    twin = core + 1 - 2 * h
    line = me // LOW
    place = lax.rem(me, LOW)
    base = line * LOW
    peers = LOW * cores
    mine = core * LOW + place
    centre = line * block + half
    bit_x = lax.rem(me, 2)
    bit_y = lax.rem(me // 2, 2)
    flip_x = 1 - 2 * bit_x
    flip_y = 2 - 4 * bit_y
    first = me + flip_x * (1 - h) + flip_y * h
    second = me + flip_y * (1 - h) + flip_x * h
    corner = me + flip_x + flip_y
    owner = place // 2 == h
    local = lax.rem(place, 2)

    barrier = pltpu.get_barrier_semaphore()

    def greet(c, b):
        pl.semaphore_signal(barrier, inc=1, device_id={"src": c, "brick": b}, device_id_type=MESH)

    def peer(k):
        t = lax.rem(mine + k, peers)
        return t // LOW, base + lax.rem(t, LOW), lax.rem(t, LOW)

    for k in range(1, peers):
        c, b, _ = peer(k)
        greet(c, b)
    for k in range(1, reach + 1):
        pl.when(line >= k)(lambda k=k: greet(core, me - LOW * k))
        pl.when(line + k < lines)(lambda k=k: greet(core, me + LOW * k))

    stations = [
        pltpu.make_async_copy(src, dst, in_sem.at[k])
        for k, (src, dst) in enumerate(((stx_ref, stx_buf), (sty_ref, sty_buf), (stz_ref, stz_buf)))
    ]
    spots = [
        pltpu.make_async_copy(src, dst, in_sem.at[3 + k])
        for k, (src, dst) in enumerate(((sx_ref, sx_buf), (sy_ref, sy_buf), (sz_ref, sz_buf)))
    ]
    seen_copy = pltpu.make_async_copy(obs_ref, seen_buf, in_sem.at[6])
    for load in stations:
        load.start()

    @pl.when(owner)
    def _():
        for load in spots:
            load.start()
        seen_copy.start()

    subs = brick_recv.shape[1]
    unit_depth = half_depth // subs

    def piece(q, part_of, u):
        return full_ref.at[pl.ds(q * depth + part_of * half_depth + u * unit_depth, unit_depth)]

    def mine_of(u):
        return slow_ref.at[pl.ds(h * half_depth + u * unit_depth, unit_depth)]

    def copy(kind, q, u, brick, own=False):
        src = mine_of(u) if own else piece(q, h, u)
        return remote(src, piece(q, h, u), brick_send.at[kind, q, u], brick_recv.at[q, u], core, brick)

    def twin_copy(q, u):
        return remote(piece(q, h, u), piece(q, h, u), brick_send.at[2, q, u], twin_sem.at[q, u], twin, me)

    def along(k, u, up):
        brick = me + LOW * k if up else me - LOW * k
        return remote(
            mine_of(u), piece(me, h, u), line_sem.at[int(up), k, u], brick_recv.at[me, u], core, brick
        )

    def own_line(k, u, wait):
        def go(up):
            c = along(k, u, up)
            c.wait_send() if wait else c.start()

        pl.when(line >= k)(lambda: go(False))
        pl.when(line + k < lines)(lambda: go(True))

    def sends(q, u, own, wait):
        for kind, brick in ((0, first), (1, second)):
            c = copy(kind, q, u, brick, own)
            c.wait_send() if wait else c.start()

    own_copy = pltpu.make_async_copy(slow_ref, full_ref.at[pl.ds(me * depth, depth)], own_sem)
    seen_send = remote(obs_ref, seen_buf, word_send.at[0], word_recv.at[0], twin, me)
    spot_send = remote(spot_ref, spot_ref, word_send.at[1], word_recv.at[1], twin, me)

    near = jnp.minimum(line, reach) + jnp.minimum(lines - 1 - line, reach)
    pl.semaphore_wait(barrier, near + peers - 1)
    pl.when(owner)(seen_send.start)
    for u in range(subs):
        own_line(1, u, False)
        sends(me, u, True, False)
        if early:
            copy(3, me, u, corner, True).start()
    for k in range(2, reach + 1):
        for u in range(subs):
            own_line(k, u, False)
    own_copy.start()

    def arrived(q, u):
        remote(
            piece(q, h, u), piece(q, h, u), brick_send.at[0, q, u], brick_recv.at[q, u], core, first
        ).wait_recv()

    def on_line(base_of, i, act):
        pl.when((i <= reach) & (line >= i))(lambda: act(base_of - LOW * i))
        pl.when((i <= reach) & (line + i < lines))(lambda: act(base_of + LOW * i))

    def both(base_of, i, act):
        pl.when(i == 0)(lambda: act(base_of))
        pl.when(i > 0)(lambda: on_line(base_of, i, act))

    def is_far(i):
        return ((i == reach) | (i == 0)) & early

    def from_line(wait, i, u):
        def act(q):
            if not wait:
                arrived(q, u)
            sends(q, u, False, wait)

            @pl.when(is_far(i))
            def _():
                c = copy(3, q, u, corner)
                c.wait_send() if wait else c.start()

            c = twin_copy(q, u)
            c.wait_send() if wait else c.start()

        return act

    def from_first(wait, i, u):
        def act(q):
            if not wait:
                arrived(q, u)

            @pl.when(jnp.logical_not(is_far(i)))
            def _():
                c = copy(1, q, u, second)
                c.wait_send() if wait else c.start()

            c = twin_copy(q, u)
            c.wait_send() if wait else c.start()

        return act

    def from_second(wait, u):
        def act(q):
            if not wait:
                arrived(q, u)
            c = twin_copy(q, u)
            c.wait_send() if wait else c.start()

        return act

    def line_turn(i, wait):
        @pl.loop(0, subs)
        def _(u):
            on_line(me, i, from_line(wait, i, u))

    def side_turn(i, wait, with_line=False):
        @pl.loop(0, subs)
        def _(u):
            if with_line:
                on_line(me, i, from_line(wait, i, u))
            both(first, i - 1, from_first(wait, i - 1, u))
            both(second, i - 1, from_second(wait, u))
            pl.when(i >= 2)(lambda: both(corner, i - 2, from_second(wait, u)))

    def corner_turn(i):
        @pl.loop(0, subs)
        def _(u):
            both(corner, i, from_second(False, u))

    @pl.when(owner)
    def _():
        for load in spots:
            load.wait()
        sub = lax.broadcasted_iota(jnp.int32, spot_ref.shape, 0)
        spot_ref[...] = jnp.where(
            sub == 0, sx_buf[local], jnp.where(sub == 1, sy_buf[local], sz_buf[local])
        )

    for load in stations:
        load.wait()
    sty = sty_buf[...]
    stz = stz_buf[...]
    stx = stx_buf[...]
    away = stx - centre
    away = jnp.where(away < 0, away + grid_x, away)
    beyond = away < ring
    step_x = jnp.where(beyond, away, grid_x - 1 - away)
    row = (step_x * rows + (sty & (rows - 1))) * 8 + (sty >> shift)
    column = jnp.where(beyond, cells_z - 1 - (stz >> 1), stz >> 1)
    column = jnp.where(((stx + sty + stz) & 1) == h, column, -1)
    code_ref[0] = row
    code_ref[1] = column
    load_code = pltpu.make_async_copy(code_ref.at[0], code, code_sem)
    load_code.start()
    rec = row.shape[1]
    hit = lax.broadcasted_iota(jnp.int32, (cells_z, rec), 0) == column

    pl.when(owner)(seen_copy.wait)
    pl.when(owner)(spot_send.start)
    pl.when(jnp.logical_not(owner))(seen_send.wait_recv)
    seen = seen_buf[pl.ds(local, 1), :] * (1.0 / spacing)
    hi = seen.astype(jnp.bfloat16).astype(jnp.float32)
    rest = seen - hi
    mid = rest.astype(jnp.bfloat16).astype(jnp.float32)
    lo = rest - mid
    for n, value in enumerate((jnp.ones_like(seen), hi, mid, lo)):
        table[pl.ds(n * cells_z, cells_z), :] = jnp.where(hit, value, 0.0).astype(jnp.bfloat16)

    tiles = TALLY // 8
    blocks = tally_ref.shape[1] // tiles

    def tally(step):
        rows_of = lax.broadcasted_iota(jnp.int32, (TALLY, rec), 0) + step * TALLY
        pick = jnp.where(rows_of == row, 1.0, 0.0).astype(jnp.bfloat16)
        got = lax.dot_general(
            pick, table[...], (((1,), (1,)), ((), ())), preferred_element_type=jnp.float32
        )
        spot = pl.ds(step * tiles, tiles)
        tally_ref[0, spot] = got[:, :cells_z].reshape(tiles, 8, cells_z)
        total = got[:, cells_z : 2 * cells_z] + (
            got[:, 2 * cells_z : 3 * cells_z] + got[:, 3 * cells_z :]
        )
        tally_ref[1, spot] = total.reshape(tiles, 8, cells_z)

    tally_send = remote(
        tally_ref.at[pl.ds(0, 2)], tally_ref.at[pl.ds(2, 2)], word_send.at[2], word_recv.at[2], twin, me
    )

    def twin_in(q):
        for u in range(subs):
            remote(
                piece(q, 1 - h, u), piece(q, 1 - h, u), brick_send.at[2, q, u], twin_sem.at[q, u], twin, me
            ).wait_recv()

    def twins(low, high):
        for i in range(low, high + 1):
            for base_of in (me, first, second, corner):
                if i:
                    on_line(base_of, i, twin_in)
                elif base_of is not me:
                    twin_in(base_of)

    if early:

        @pl.loop(0, blocks)
        def _(step):
            tally(step)

            @pl.when(step == 0)
            def _():
                line_turn(1, False)
                side_turn(1, False)

        side_turn(reach, False)
        line_turn(reach, False)

        for gap in range(reach + 1, lines):
            for away_line in (line - gap, line + gap):

                @pl.when((away_line >= 0) & (away_line < lines))
                def _():
                    @pl.loop(0, block)
                    def _(x):
                        full_ref[away_line * block + x] = jnp.ones((cells_y, cells_z), jnp.float32)

    else:

        @pl.loop(0, max(reach + 2, blocks))
        def _(step):
            pl.when(step < reach + 2)(lambda: side_turn(step + 1, False, True))
            pl.when(step < blocks)(lambda: tally(step))

    own_copy.wait()
    tally_send.start()
    twins(0, 0 if early else reach)

    share = got_ref.shape[-1]
    quarter = picked.shape[0]
    pl.when(jnp.logical_not(owner))(spot_send.wait_recv)
    keep = slots_ref.shape[2]
    for t in range(depth):
        own_ref[t] = full_ref[me * depth + t, pl.ds(pl.multiple_of(core * keep, 8), keep), :]

    picks = ((line > 0) & (line < lines - 1)) if early else line >= 0

    def pick_line(n):
        if not early:
            return line
        return (line - 1) * 2 + n

    lane = lax.broadcasted_iota(jnp.int32, (8, cells_z), 1)
    sub = lax.broadcasted_iota(jnp.int32, (8, cells_z), 0)
    sub_first = sub == 0
    sub_last = sub == 7
    upper = lane >= half_z
    inner = jnp.where(upper, cells_z - 1 - lane, lane)
    parity = [lax.rem(q + h, 2) for q in range(2)]
    cell_z = [inner * 2 + jnp.where(upper, 1 - p, p) for p in parity]
    from_low = [(lane & 1) == p for p in parity]
    edge_z = [(lane & (half_z - 1)) == p * (half_z - 1) for p in parity]
    slide = [1 + p * (cells_z - 2) for p in parity]
    mirror = cells_z - 1 - lane

    def slot(i, v):
        return (i + 1) * rows + v

    sx = spot_ref[0:1, :]
    sy = spot_ref[1:2, :]
    sz = spot_ref[2:3, :]
    unit = (start_slowness * spacing) ** 2
    flat = []
    for q in range(2):
        dz = (cell_z[q] - sz).astype(jnp.float32)
        dz = dz * dz
        for v in range(rows):
            dy = (sub * rows + v - sy).astype(jnp.float32)
            flat.append((dy * dy + dz) * unit)

    def prepare(quad):
        for j in range(4):
            i = quad * 4 + j
            x_low = centre - 1 - i
            x_low = jnp.where(x_low < 0, x_low + grid_x, x_low)
            x_high = centre + i
            x_high = jnp.where(x_high >= grid_x, x_high - grid_x, x_high)
            dx = (jnp.where(upper, x_high, x_low) - sx).astype(jnp.float32)
            dx = dx * dx * unit
            for v in range(rows):
                q = (j + 1 + v) % 2
                low = full_ref[x_low, pl.ds(v, 8, stride=rows), :]
                high = full_ref[x_high, pl.ds(v, 8, stride=rows), :]
                pair_of = (
                    (chain, chain_cost, q, jnp.where(from_low[q], low, high)),
                    (other, other_cost, 1 - q, jnp.where(from_low[q], high, low)),
                )
                for field, cost, k, natural in pair_of if q else pair_of[::-1]:
                    slow = jnp.take_along_axis(natural, cell_z[k], axis=1)
                    square = dx + flat[k * rows + v]
                    start = square * lax.rsqrt(jnp.maximum(square, unit * 0.5))
                    cost[i * rows + v] = (2.0 * half_step) * slow
                    field[slot(i, v)] = start + half_step * slow

    @pl.loop(0, (half if early else ring) // 4)
    def _(quad):
        prepare(quad)

    cuts = {
        b: jnp.where(upper, grid_x - centre, centre) == b for b in range(half, ring, half) if (b // half) % 2
    }

    def swing(one):
        return jnp.take_along_axis(one, mirror, axis=1)

    def across_z(one, k):
        return pltpu.roll(one, slide[k], 1)

    def y_up(cur, v):
        return cur[v + 1] if v + 1 < rows else pltpu.roll(cur[0], 7, 0)

    def y_down(cur, v):
        return cur[v - 1] if v else pltpu.roll(cur[rows - 1], 1, 0)

    def layer_of(ref, i):
        return [ref[slot(i, v)] for v in range(rows)]

    def sweep(dst, cost, src, turned, low_end, high_end):
        cur = layer_of(src, low_end)
        prev = layer_of(src, low_end - 1) if low_end else [swing(one) for one in cur]
        for i in range(low_end, high_end):
            after_of = layer_of(src, i + 1) if i + 1 < ring else [swing(one) for one in cur]
            for v in range(rows):
                q = (i + 1 + v) % 2
                before = prev[v]
                after = after_of[v]
                if i in cuts:
                    before = jnp.where(cuts[i], big_value, before)
                if i + 1 in cuts:
                    after = jnp.where(cuts[i + 1], big_value, after)
                up = y_up(cur, v)
                down = y_down(cur, v)
                if v + 1 == rows:
                    up = jnp.where(sub_last, big_value, up)
                if v == 0:
                    down = jnp.where(sub_first, big_value, down)
                k = q ^ turned
                across = jnp.where(edge_z[k], cur[v], across_z(cur[v], k))
                low = jnp.minimum(across, cur[v])
                for value in (before, after, down, up):
                    low = jnp.minimum(low, value)
                dst[slot(i, v)] = jnp.minimum(dst[slot(i, v)], low + cost[i * rows + v])
            prev, cur = cur, after_of

    assert ITERS % 2 == 0

    def step_of(j, low_end, high_end):
        if j % 2:
            sweep(other, other_cost, chain, 1, low_end, high_end)
        else:
            sweep(chain, chain_cost, other, 0, low_end, high_end)

    stops = [0, 1 + half, 1 + 2 * half, 1 + span]
    time_copies = []
    for n, (low, high) in enumerate(zip(stops, stops[1:])):
        part_of = pl.ds(low * rows, (high - low) * rows)
        time_copies.append(
            remote(chain.at[part_of], twin_time.at[part_of], time_send.at[n], time_recv.at[n], twin, me)
        )

    def scale_times(low_end, high_end):
        if low_end == 0:
            for v in range(rows):
                one = (chain[slot(0, v)] - 0.5 * chain_cost[v]) * (1.0 / spacing)
                chain[slot(-1, v)] = swing(one)

        @pl.loop(low_end, high_end)
        def _(i):
            for v in range(rows):
                chain[slot(i, v)] = (chain[slot(i, v)] - 0.5 * chain_cost[i * rows + v]) * (1.0 / spacing)

    if early:
        assert reach == 2 and span == 3 * half

        def stage(done, ready, hook=None):
            for j in range(1, ITERS + 1):
                low_end = max(done - j, 0)
                high_end = ready if ready == ring else ready - j
                if high_end > low_end:
                    step_of(j, low_end, high_end)
                if hook is not None and j == ITERS // 2:
                    hook()

        stage(0, half)
        corner_turn(reach - 1)
        twins(1, reach - 1)

        @pl.loop(half // 4, span // 4)
        def _(quad):
            prepare(quad)

        def relay_far():
            @pl.loop(0, subs)
            def _(u):
                both(first, reach, from_first(False, reach, u))
                both(second, reach, from_second(False, u))

        stage(half, span, relay_far)
        scale_times(0, half)
        corner_turn(reach)
        time_copies[0].start()
        twins(reach, reach)

        @pl.loop(span // 4, ring // 4)
        def _(quad):
            prepare(quad)

        stage(span, ring)
    else:

        @pl.loop(0, ITERS // 2)
        def _(_step):
            step_of(1, 0, ring)
            step_of(2, 0, ring)

    if not early:
        scale_times(0, half)
        time_copies[0].start()
    scale_times(half, ring)
    for copy_of in time_copies[1:]:
        copy_of.start()

    load_code.wait()
    unroll = 16

    def pick_rows(n, low_end, high_end):
        place_of = pl.multiple_of(pick_line(n) * quarter, 128)

        @pl.loop(low_end // unroll, high_end // unroll)
        def _(m):
            for j in range(unroll):
                r = m * unroll + j
                at = code[0, place_of + r]
                picked[pl.ds(r, 1), :] = chain[(at >> 3) + rows, pl.ds(at & 7, 1), :]

    def pick(n, low_end):
        pick_rows(n, low_end, quarter)
        place_of = pl.multiple_of(pick_line(n) * quarter, 128)
        column = code_ref[1, :, pl.ds(place_of, quarter)]
        turned = jnp.transpose(picked[...])
        here = lax.broadcasted_iota(jnp.int32, turned.shape, 0) == column
        arrived_at = jnp.sum(jnp.where(here, turned, 0.0), axis=0, keepdims=True) * spacing
        for k in range(LOW):
            part[n * LOW + k] = arrived_at[:, k * share : (k + 1) * share]

    for v in range(rows):
        chain_field[slot(span - 2, v)] = jnp.zeros((8, cells_z), jnp.float32)
        chain_field[slot(span - 1, v)] = jnp.zeros((8, cells_z), jnp.float32)
        chain_field[slot(span, v)] = jnp.zeros((8, cells_z), jnp.float32)
        other_field[slot(span, v)] = jnp.zeros((8, cells_z), jnp.float32)

    bound = jnp.where(upper, grid_x - centre, centre)
    tally_send.wait_recv()

    def weigh(at, i, own, theirs, weight, supply, field, tally, turned):
        cur = [theirs[slot(at, v)] for v in range(rows)]
        cut_before = bound == at
        cut_after = bound == at + 1
        for v in range(rows):
            q = (i + 1 + v) % 2
            one = own[slot(at, v)]

            def gain(value):
                return jnp.maximum(value - one, 0.0)

            before = gain(theirs[slot(at - 1, v)])
            after = gain(theirs[slot(at + 1, v)])
            if i % half == 0:
                before = jnp.where(cut_before, 0.0, before)
            if (i + 1) % half == 0:
                after = jnp.where(cut_after, 0.0, after)
            up = gain(y_up(cur, v))
            down = gain(y_down(cur, v))
            if v + 1 == rows:
                up = jnp.where(sub_last, 0.0, up)
            if v == 0:
                down = jnp.where(sub_first, 0.0, down)
            k = q ^ turned
            across = jnp.where(edge_z[k], 0.0, gain(across_z(cur[v], k)))
            parts = (before, after, down, up, gain(cur[v]), across)
            total = ((parts[0] + parts[1]) + (parts[2] + parts[3])) + (parts[4] + parts[5])
            inverse = 1.0 / (1.0 + total)
            spot = at * rows + v
            for n, gained in enumerate(parts):
                weight[n, spot] = gained * inverse
            value = (tally_ref[tally, spot] * one - tally_ref[tally + 1, spot]) * inverse
            supply[spot] = value
            if turned:
                field[slot(at, v)] = value

    def weigh_both(at, i):
        weigh(at, i, twin_time, chain, other_weight, other_supply, other_field, 2, 1)
        weigh(at, i, chain, twin_time, chain_weight, chain_supply, chain_field, 0, 0)

    time_copies[0].wait_recv()
    for i in range(half - 1):
        weigh_both(i, i)
    pl.when(picks)(lambda: pick_rows(0, 0, quarter // 2))

    @pl.loop(0, span // half - 1)
    def _(chunk):
        for n, copy_of in enumerate(time_copies[1:]):
            pl.when(chunk == n)(copy_of.wait_recv)
        for i in range(half - 1, 2 * half - 1):
            weigh_both(chunk * half + i, i)

    for v in range(rows):
        other_field[slot(-1, v)] = swing(other_field[slot(0, v)])

    def backward(count, dst, weight, supply, src, turned):
        cur = layer_of(src, 0)
        prev = [swing(one) for one in cur]
        for i in range(count):
            after_of = layer_of(src, i + 1)
            for v in range(rows):
                q = (i + 1 + v) % 2
                spot = i * rows + v
                acc = supply[spot] + weight[0, spot] * prev[v]
                acc = acc + weight[1, spot] * after_of[v]
                side = weight[2, spot] * y_down(cur, v) + weight[3, spot] * y_up(cur, v)
                across = across_z(cur[v], q ^ turned)
                acc = (acc + side) + (weight[4, spot] * cur[v] + weight[5, spot] * across)
                dst[slot(i, v)] = acc
            prev, cur = cur, after_of

    def rounds(first_sweep, times):
        count = half + ITERS - first_sweep

        @pl.loop(0, times)
        def _(_step):
            backward(count, chain_field, chain_weight, chain_supply, other_field, 0)
            backward(count - 1, other_field, other_weight, other_supply, chain_field, 1)

    rounds(2, 3)
    rounds(8, 2)
    rounds(12, 2)
    backward(half, chain_field, chain_weight, chain_supply, other_field, 0)

    for k in range(LOW):
        for t in range(0, depth, 2):
            low_side = k < LOW // 2
            near, next_to = (
                (half - 1 - (k * depth + t + n)) if low_side else (k * depth + t + n - half) for n in range(2)
            )
            for v in range(rows):
                a = chain_field[slot(near, v)]
                b = chain_field[slot(next_to, v)]
                merged = jnp.where(upper, swing(b), a) if low_side else jnp.where(upper, b, swing(a))
                packed[k, t // 2, pl.ds(v, 8, stride=rows), :] = merged

    keep = slots_ref.shape[2]

    def ship(k):
        c, b, p = peer(k)
        return remote(
            packed.at[p, :, pl.ds(c * keep, keep)], slots_ref.at[mine], send_sem.at[k], recv_sem.at[mine], c, b
        )

    for k in range(1, peers):
        ship(k).start()
    stay = pltpu.make_async_copy(
        packed.at[place, :, pl.ds(core * keep, keep)], slots_ref.at[mine], self_sem
    )
    stay.start()

    target = core - h + place // 2

    def word(n, k):
        return remote(
            part.at[n * LOW + k],
            got_ref.at[local, h],
            part_send.at[n * LOW + k],
            part_recv.at[local, h],
            target,
            pick_line(n) * LOW + k,
        )

    def home(n, k):
        return (target == core) & (pick_line(n) * LOW + k == me)

    def post(n):
        for k in range(LOW):
            pl.when(jnp.logical_not(home(n, k)))(word(n, k).start)

            @pl.when(home(n, k))
            def _():
                got_ref[local, h] = part[n * LOW + k]

    def posted(n):
        for k in range(LOW):
            pl.when(jnp.logical_not(home(n, k)))(word(n, k).wait_send)

    pl.when(picks)(lambda: pick(0, quarter // 2))
    pl.when(picks)(lambda: post(0))
    if early:
        pl.when(picks)(lambda: pick(1, 0))
        pl.when(picks)(lambda: post(1))

    for copy_of in time_copies:
        copy_of.wait_send()
    tally_send.wait_send()
    for u in range(subs):
        sends(me, u, True, True)
        if early:
            copy(3, me, u, corner, True).wait_send()
        for k in range(1, reach + 1):
            own_line(k, u, True)

    @pl.loop(1, reach + 3)
    def _(i):
        side_turn(i, True, True)

    @pl.when(owner)
    def _():
        seen_send.wait_send()
        spot_send.wait_send()

    def word_in(n, side):
        return remote(
            part.at[0], got_ref.at[n, side], part_send.at[0], part_recv.at[n, side], core, me
        )

    for n in range(2):
        for side in range(2):
            from_me = picks & (place == 2 * h + n) & (h == side)
            pl.when(jnp.logical_not(from_me))(word_in(n, side).wait_recv)
    for k in range(1, peers):
        m = lax.rem(mine + k, peers)
        remote(
            packed.at[0, :, pl.ds(0, keep)], slots_ref.at[m], send_sem.at[k], recv_sem.at[m], core, me
        ).wait_recv()
    for k in range(1, peers):
        ship(k).wait_send()
    pl.when(picks)(lambda: posted(0))
    if early:
        pl.when(picks)(lambda: posted(1))
    stay.wait()


def finish_kernel(cores, slots_ref, got_ref, own_ref, out_ref, arr_ref):
    depth, keep, cells_z = out_ref.shape
    half_z = cells_z // 2
    lane = lax.broadcasted_iota(jnp.int32, (8, cells_z), 1)
    sub = lax.broadcasted_iota(jnp.int32, (8, cells_z), 0)
    upper = lane >= half_z
    plain = ((sub + jnp.where(upper, 1, 0)) & 1) == 0
    join = jnp.where((lane & 1) == 0, lane >> 1, cells_z - 1 - (lane >> 1))
    mirror = cells_z - 1 - lane
    for t in range(depth // 2):
        for y in range(0, keep, 8):
            sums = []
            for colour in range(2):
                total = None
                for c in range(colour, cores, 2):
                    for k in range(LOW):
                        one = slots_ref[c * LOW + k, t, pl.ds(y, 8), :]
                        total = one if total is None else total + one
                sums.append(total)
            even = jnp.where(plain, sums[0], sums[1])
            odd = jnp.where(plain, sums[1], sums[0])
            moved = jnp.take_along_axis(jnp.where(upper, even, odd), mirror, axis=1)
            for n, packed in enumerate((jnp.where(upper, moved, even), jnp.where(upper, odd, moved))):
                value = jnp.take_along_axis(packed, join, axis=1)
                slow = own_ref[2 * t + n, pl.ds(y, 8), :]
                out_ref[2 * t + n, pl.ds(y, 8), :] = (slow * spacing) * value
    for n in range(2):
        arr_ref[pl.ds(n, 1), :] = got_ref[n, 0] + got_ref[n, 1]


def per_device(slowness, source_x, source_y, source_z, station_x, station_y, station_z, observed):
    bricks = lax.axis_size("brick")
    cores = lax.axis_size("src")
    depth, cells_y, cells_z = slowness.shape
    grid_x = depth * bricks
    rec = station_x.shape[0]
    rows = cells_y // 8
    ring = grid_x // 2
    half = LOW * depth // 2
    span = half + ITERS
    assert source_x.shape[0] == 2 and bricks % LOW == 0 and cores % 2 == 0
    assert half % 2 == 0 and span % half == 0 and span + 1 <= ring and (span * rows * 8) % TALLY == 0
    assert span % 4 == 0 and ring % 4 == 0
    f32 = jnp.float32
    i32 = jnp.int32
    share = rec // bricks
    quarter = share * LOW
    keep = cells_y // cores
    ring_shape = ((ring + 2) * rows, 8, cells_z)
    span_shape = ((span + 2) * rows, 8, cells_z)
    dma = pltpu.SemaphoreType.DMA
    subs = 1
    slots, got, own = pl.pallas_call(
        functools.partial(solve_kernel, bricks, cores),
        name="solve",
        out_shape=(
            jax.ShapeDtypeStruct((LOW * cores, depth // 2, keep, cells_z), f32),
            jax.ShapeDtypeStruct((2, 2, 1, share), f32),
            jax.ShapeDtypeStruct((depth, keep, cells_z), f32),
        ),
        in_specs=[HBM] * 8,
        out_specs=(VMEM, VMEM, VMEM),
        scratch_shapes=[
            pltpu.VMEM((grid_x, cells_y, cells_z), f32),
            pltpu.VMEM((4, span * rows, 8, cells_z), f32),
            pltpu.VMEM((2, 1, rec), i32),
            pltpu.VMEM((8, cells_z), i32),
            pltpu.VMEM((4 * cells_z, rec), jnp.bfloat16),
            pltpu.VMEM(ring_shape, f32),
            pltpu.VMEM(ring_shape, f32),
            pltpu.VMEM((ring * rows, 8, cells_z), f32),
            pltpu.VMEM((ring * rows, 8, cells_z), f32),
            pltpu.VMEM(span_shape, f32),
            pltpu.VMEM((6, span * rows, 8, cells_z), f32),
            pltpu.VMEM((6, span * rows, 8, cells_z), f32),
            pltpu.VMEM((span * rows, 8, cells_z), f32),
            pltpu.VMEM((span * rows, 8, cells_z), f32),
            pltpu.VMEM(span_shape, f32),
            pltpu.VMEM(span_shape, f32),
            pltpu.VMEM((LOW, depth // 2, cells_y, cells_z), f32),
            pltpu.VMEM((quarter, cells_z), f32),
            pltpu.VMEM((2 * LOW, 1, share), f32),
            pltpu.VMEM((1, rec), i32),
            pltpu.VMEM((1, rec), i32),
            pltpu.VMEM((1, rec), i32),
            pltpu.VMEM(observed.shape, f32),
            pltpu.SMEM((1, rec), i32),
            pltpu.SMEM((2,), i32),
            pltpu.SMEM((2,), i32),
            pltpu.SMEM((2,), i32),
            dma((2, bricks // LOW, subs)),
            dma((4, bricks, subs)),
            dma((bricks, subs)),
            dma((bricks, subs)),
            dma,
            dma((7,)),
            dma((3,)),
            dma((3,)),
            dma,
            dma((span // half,)),
            dma((span // half,)),
            dma((LOW * cores,)),
            dma((LOW * cores,)),
            dma((2 * LOW,)),
            dma((2, 2)),
            dma,
        ],
        compiler_params=pltpu.CompilerParams(
            collective_id=0, has_side_effects=True, vmem_limit_bytes=SOLVE_VMEM
        ),
    )(
        *(
            pltpu.with_memory_space_constraint(a, pltpu.HBM)
            for a in (
                slowness,
                source_x,
                source_y,
                source_z,
                station_x[None],
                station_y[None],
                station_z[None],
                observed,
            )
        )
    )

    return tuple(
        pl.pallas_call(
            functools.partial(finish_kernel, cores),
            name="finish",
            out_shape=(
                jax.ShapeDtypeStruct((depth, keep, cells_z), f32),
                jax.ShapeDtypeStruct((2, share), f32),
            ),
            in_specs=[VMEM] * 3,
            compiler_params=pltpu.CompilerParams(vmem_limit_bytes=FINISH_VMEM),
        )(slots, got, own)
    )


def solution(mesh):
    in_specs = (P("brick", None, None), P("src"), P("src"), P("src"), P(), P(), P(), P("src", None))
    out_specs = (P("brick", "src", None), P("src", "brick"))
    return jax.shard_map(
        per_device, mesh=mesh, in_specs=in_specs, out_specs=out_specs, check_vma=False
    )
```
